32 devices in a mesh: row: 8 (over z, core), loop: 4 (over y, x).
Axes of the slice: x: 2, y: 2, z: 4, core: 2. Of those that a mesh axis runs over, the one named last changes fastest.
Arguments:
- student_image: bfloat16 [5120, 1024], P(('row', 'loop')), may hold values from -12 to 12
- student_text: bfloat16 [5120, 1024], P(('row', 'loop')), may hold values from -12 to 12
- teacher_image: bfloat16 [5120, 1024], P('row', 'loop'), may hold values from -12 to 12
- teacher_text: bfloat16 [5120, 1024], P('row', 'loop'), may hold values from -12 to 12
- student_scale: float32 [1], replicated, may hold values from 30 to 100
- teacher_scale: float32 [1], replicated, may hold values from 30 to 100
Outputs:
- loss: float32 [1], replicated
- grad_image: bfloat16 [5120, 1024], P(('row', 'loop'))
- grad_text: bfloat16 [5120, 1024], P(('row', 'loop'))
The draws below stay inside these ranges and needn't reach their ends.
All inputs are finite; a program needn't handle non-finite values.
Results may differ from the reference program's by a relative error of at most 0.014.
The reference program's roundings to bfloat16 on the way (of `simg` and `grad_logits`) count: a program that leaves them out, or rounds other values in their place, can miss the bound.
Values may be sent and summed in bfloat16 or wider, within the bound.
A program may use at most 128 MiB of HBM per device.

```python
import math
import jax
import jax.numpy as jnp
from jax import lax

CODE = 1024
ROWS_DEV = 160
BATCH = 5120
ROW_BLOCK = 640
N_ROW = 8
N_LOOP = 4


def raw_codes(key, stream):
    base_key = jax.random.fold_in(key, stream)
    first = jax.random.normal(jax.random.fold_in(base_key, 1), (BATCH, CODE), jnp.float32)
    second = jax.random.normal(jax.random.fold_in(base_key, 2), (BATCH, CODE), jnp.float32)
    return (first, second)


def blend_weights():
    groups = BATCH // ROW_BLOCK
    group = (jnp.arange(BATCH, dtype=jnp.int32) // ROW_BLOCK).astype(jnp.float32)
    frac = group / float(max(groups - 1, 1))
    theta = 0.1 + (0.5 * math.pi - 0.1) * frac
    return (jnp.cos(theta)[:, None], jnp.sin(theta)[:, None])


def pair_codes(key, stream):
    teach_img, teach_txt = raw_codes(key, 202)
    if stream == 202:
        images, text_rows = (teach_img, teach_txt)
    else:
        own_img, own_txt = raw_codes(key, 101)
        near, far = blend_weights()
        images = near * teach_img + far * own_img
        text_rows = near * teach_txt + far * own_txt
    return (jnp.clip(images, -6.0, 6.0), jnp.clip(text_rows, -6.0, 6.0))


def logit_scales(key):
    scale_key = jax.random.fold_in(key, 300)
    student = jnp.exp(jax.random.uniform(jax.random.fold_in(scale_key, 1), (1,), jnp.float32, math.log(30.0), math.log(100.0)))
    factor = jnp.exp(jax.random.uniform(jax.random.fold_in(scale_key, 2), (1,), jnp.float32, -0.1, 0.1))
    teacher = jnp.clip(student * factor, 30.0, 100.0)
    return (student, teacher)


def draw_student_image(key, part):
    return pair_codes(key, 101)[0].astype(jnp.bfloat16)


def draw_student_text(key, part):
    return pair_codes(key, 101)[1].astype(jnp.bfloat16)


def draw_teacher_image(key, part):
    return pair_codes(key, 202)[0].astype(jnp.bfloat16)


def draw_teacher_text(key, part):
    return pair_codes(key, 202)[1].astype(jnp.bfloat16)


def draw_student_scale(key, part):
    return logit_scales(key)[0]


def draw_teacher_scale(key, part):
    return logit_scales(key)[1]


def setup_inputs(seed: int = 0) -> dict:
    key_of = jax.random.split(jax.random.key(seed), 7)
    student_image = draw_student_image(jax.random.fold_in(key_of[6], 71), 0)
    student_text = draw_student_text(jax.random.fold_in(key_of[6], 71), 0)
    teacher_image = draw_teacher_image(jax.random.fold_in(key_of[6], 71), 0)
    teacher_text = draw_teacher_text(jax.random.fold_in(key_of[6], 71), 0)
    student_scale = draw_student_scale(jax.random.fold_in(key_of[6], 71), 0)
    teacher_scale = draw_teacher_scale(jax.random.fold_in(key_of[6], 71), 0)
    return dict(student_image=student_image, student_text=student_text, teacher_image=teacher_image, teacher_text=teacher_text, student_scale=student_scale, teacher_scale=teacher_scale)


EPS = 1e-06

def unit_rows(codes):
    values = codes.astype(jnp.float32)
    norms = jnp.sqrt(lax.optimization_barrier(jnp.sum(values * values, axis=1, keepdims=True)) + EPS)
    return (values / norms, norms)

def back_norm(grad_unit, units, norms):
    inner = lax.optimization_barrier(jnp.sum(grad_unit * units, axis=1, keepdims=True))
    return ((grad_unit - units * inner) / norms).astype(jnp.bfloat16)

def rounded_term(term):
    narrow = lax.optimization_barrier(term.astype(jnp.bfloat16))
    return narrow.astype(jnp.float32)

def reference(student_image, student_text, teacher_image, teacher_text, student_scale, teacher_scale):
    simg_unit, simg_norm = unit_rows(student_image)
    stxt_unit, stxt_norm = unit_rows(student_text)
    simg = simg_unit.astype(jnp.bfloat16)
    stxt = stxt_unit.astype(jnp.bfloat16)
    timg = unit_rows(teacher_image)[0].astype(jnp.bfloat16)
    ttxt = unit_rows(teacher_text)[0].astype(jnp.bfloat16)
    sscale = student_scale[0]
    tscale = teacher_scale[0]
    block = ROWS_DEV * N_LOOP
    count = BATCH // block
    stxt_split = stxt.reshape(N_ROW, N_LOOP, ROWS_DEV, CODE)

    def one_block(carry, index):
        total, text_acc = carry
        start = (index * block).astype(jnp.int32)
        simg_b = lax.dynamic_slice_in_dim(simg, start, block, 0)
        timg_b = lax.dynamic_slice_in_dim(timg, start, block, 0)
        slog = sscale * jnp.dot(simg_b, stxt.T, preferred_element_type=jnp.float32)
        tlog = tscale * jnp.dot(timg_b, ttxt.T, preferred_element_type=jnp.float32)
        lses = jax.nn.logsumexp(slog, axis=1)
        lset = jax.nn.logsumexp(tlog, axis=1)
        probt = jnp.exp(tlog - lset[:, None])
        probs = jnp.exp(slog - lses[:, None])
        diverge = lax.optimization_barrier(jnp.sum(probt * (tlog - slog), axis=1)) - lset + lses
        grad_logits = (sscale * (probs - probt)).astype(jnp.bfloat16)
        grad_split = grad_logits.reshape(block, N_ROW, N_LOOP, ROWS_DEV)
        dimg = jnp.zeros((block, CODE), jnp.float32)
        for column_class in range(N_LOOP):
            class_cols = grad_split[:, :, column_class, :].reshape(block, N_ROW * ROWS_DEV)
            class_text = stxt_split[:, column_class, :, :].reshape(N_ROW * ROWS_DEV, CODE)
            dimg = dimg + rounded_term(jnp.dot(class_cols, class_text, preferred_element_type=jnp.float32))
        text_term = jnp.dot(grad_logits.T, simg_b, preferred_element_type=jnp.float32)
        text_acc = text_acc + rounded_term(text_term)
        return ((total + jnp.sum(diverge), text_acc), dimg)
    start_carry = (jnp.zeros((), jnp.float32), jnp.zeros((BATCH, CODE), jnp.float32))
    (total, dtxt), dimg_blocks = lax.scan(one_block, start_carry, jnp.arange(count, dtype=jnp.int32))
    dimg = dimg_blocks.reshape(BATCH, CODE)
    loss = (total / BATCH).reshape(1)
    return (loss, back_norm(dimg, simg_unit, simg_norm), back_norm(dtxt, stxt_unit, stxt_norm))
```

```python
import functools
import jax
import jax.numpy as jnp
from jax import lax
from jax.experimental import pallas as pl
from jax.experimental.pallas import tpu as pltpu
from jax.sharding import PartitionSpec as P

EPS = 1e-06
F32 = jnp.float32
BF16 = jnp.bfloat16
MESH = pl.DeviceIdType.MESH
STEP = 32


class Ids:
    def __init__(self):
        self.table = {}
        self.count = 0

    def take(self, name, size=1):
        self.table[name] = self.count
        self.count += size

    def __getitem__(self, name):
        return self.table[name]


def make_ids(n_loop, n_kh, n_kl, n_lx, n_ly):
    ids = Ids()
    ids.take("t_img", n_loop)
    ids.take("t_txt", n_loop)
    for a in range(2):
        ids.take(("iz", a), n_kl)
        ids.take(("iy", a), n_ly * n_kl)
        ids.take(("tz", a), n_kh)
        ids.take(("tx", a), n_lx * n_kh)
        ids.take(("tc", a), n_lx * n_kh)
    ids.take("stat", n_kl * n_ly)
    ids.take("dc", n_lx * n_kh)
    ids.take("dx", n_lx * n_kh)
    ids.take("dz", n_kh)
    ids.take("gy", n_ly * n_kl)
    ids.take("gz", n_kl)
    ids.take("lk", n_kh)
    ids.take("lx", n_lx)
    ids.take("lc", 1)
    return ids


def kernel(
    dims, ids,
    si, st, ti, tt, ssc, tsc,
    loss_out, gi_out, gt_out,
    img_s, img_t, own_s, own_t, txt_s, txt_t, raw_i, raw_t,
    slog, tlog, grad, stat, dimg_acc, r1, r2, r3, ry, rz, part,
    ss, rs,
):
    n_row, n_loop, n_kh, n_kl, n_lx, n_ly, D, code = dims
    n_img = n_kl * n_ly
    n_txt = n_kh * n_lx * 2
    rows = n_img * D
    cols = n_txt * D
    feat = code // n_loop
    r = lax.axis_index("row")
    l = lax.axis_index("loop")
    k, c = r // 2, r % 2
    kh, kl = k // n_kl, k % n_kl
    src_kl, src_j = k // n_kh, k % n_kh
    ly, lx = l // n_lx, l % n_lx
    sscale = ssc[0]
    tscale = tsc[0]

    def dev(k_=None, c_=None, ly_=None, lx_=None):
        kk = k if k_ is None else k_
        cc = c if c_ is None else c_
        yy = ly if ly_ is None else ly_
        xx = lx if lx_ is None else lx_
        return (kk * 2 + cc, yy * n_lx + xx)

    def piece(ref, slot):
        return ref.at[pl.ds(pl.multiple_of(slot * D, D), D), :]

    def at(slot):
        return pl.ds(pl.multiple_of(slot * D, D), D)

    def copy(src, dst, q_send, q_recv, device):
        return pltpu.make_async_remote_copy(
            src_ref=src, dst_ref=dst, send_sem=ss.at[q_send], recv_sem=rs.at[q_recv],
            device_id=device, device_id_type=MESH,
        )

    sent = []

    def send(src, dst, q_send, q_recv, device):
        op = copy(src, dst, q_send, q_recv, device)
        op.start()
        sent.append(op)

    def got(dst, q):
        copy(dst, dst, q, q, dev(c_=1 - c)).wait_recv()

    def drain():
        for op in sent:
            op.wait_send()
        sent.clear()

    barrier = pltpu.get_barrier_semaphore()
    n_peer = 0
    for d in range(1, n_loop):
        pl.semaphore_signal(barrier, inc=1, device_id=(r, (l + d) % n_loop), device_id_type=MESH)
        n_peer += 1
    for d in range(1, n_kh * n_kl):
        pl.semaphore_signal(barrier, inc=1, device_id=dev(k_=(k + d) % (n_kh * n_kl)), device_id_type=MESH)
        n_peer += 1
    pl.semaphore_signal(barrier, inc=1, device_id=dev(c_=1 - c), device_id_type=MESH)
    n_peer += 1
    for d in range(1, n_kl):
        for e in range(1, n_ly):
            diagonal = dev(k_=kh * n_kl + (kl + d) % n_kl, ly_=(ly + e) % n_ly)
            pl.semaphore_signal(barrier, inc=1, device_id=diagonal, device_id_type=MESH)
            n_peer += 1
    pl.semaphore_wait(barrier, n_peer)

    slot0 = kl * n_ly + ly

    def islot(kl_, ly_):
        return kl_ * n_ly + ly_

    def tslot(j, lx_, c_):
        return (j * n_lx + lx_) * 2 + c_

    def inv_norm(x):
        n2 = jnp.sum(x * x, axis=1, keepdims=True) + EPS
        n = jnp.sqrt(n2)
        return n, 1.0 / n

    HALF = 32

    def unit_to(src, dst, base):
        def body(i, _):
            o = pl.multiple_of(i * HALF, HALF)
            x = src[pl.ds(o, HALF), :].astype(F32)
            _, inv = inv_norm(x)
            dst[pl.ds(pl.multiple_of(base + o, HALF), HALF), :] = (x * inv).astype(BF16)
            return 0
        lax.fori_loop(0, D // HALF, body, 0)

    def a2a(src, raw, base):
        for d in range(1, n_loop):
            peer = (l + d) % n_loop
            send(piece(src, peer), raw.at[l], base + d, base + d, (r, peer))

    def image_first(a, buf):
        for d in range(1, n_kl):
            p = (kl + d) % n_kl
            q = ids[("iz", a)] + d
            send(piece(buf, slot0), piece(buf, slot0), q, q, dev(k_=kh * n_kl + p))
        for e in range(1, n_ly):
            q = ids[("iy", a)] + e * n_kl
            send(piece(buf, slot0), piece(buf, slot0), q, q, dev(ly_=(ly + e) % n_ly))

    def image_relay(a, buf):
        for d in range(1, n_kl):
            s = islot((kl + n_kl - d) % n_kl, ly)
            got(piece(buf, s), ids[("iz", a)] + d)
            for e in range(1, n_ly):
                q = ids[("iy", a)] + e * n_kl + d
                send(piece(buf, s), piece(buf, s), q, q, dev(ly_=(ly + e) % n_ly))

    def image_finish(a, buf):
        for e in range(1, n_ly):
            for d in range(n_kl):
                s = islot((kl + n_kl - d) % n_kl, (ly + n_ly - e) % n_ly)
                got(piece(buf, s), ids[("iy", a)] + e * n_kl + d)

    def text_first(a, own, buf):
        s = tslot(src_j, lx, c)
        for h in range(n_kh):
            dest = h * n_kl + src_kl
            op = copy(own, piece(buf, s), ids[("tz", a)] + h, ids[("tz", a)] + src_j, dev(k_=dest))

            @pl.when(dest != k)
            def _():
                op.start()

            @pl.when(dest == k)
            def _():
                buf[at(s), :] = own[...]

    def text_first_drain(a, own, buf):
        s = tslot(src_j, lx, c)
        for h in range(n_kh):
            dest = h * n_kl + src_kl
            op = copy(own, piece(buf, s), ids[("tz", a)] + h, ids[("tz", a)] + src_j, dev(k_=dest))

            @pl.when(dest != k)
            def _():
                op.wait_send()

    def text_relay(a, buf):
        for j in range(n_kh):
            s = tslot(j, lx, c)

            @pl.when(kl * n_kh + j != k)
            def _():
                got(piece(buf, s), ids[("tz", a)] + j)

            for e in range(1, n_lx):
                q = ids[("tx", a)] + e * n_kh + j
                send(piece(buf, s), piece(buf, s), q, q, dev(lx_=(lx + e) % n_lx))
            q = ids[("tc", a)] + j
            send(piece(buf, s), piece(buf, s), q, q, dev(c_=1 - c))

    def text_cross(a, buf):
        for e in range(1, n_lx):
            for j in range(n_kh):
                s = tslot(j, (lx + n_lx - e) % n_lx, c)
                got(piece(buf, s), ids[("tx", a)] + e * n_kh + j)
                q = ids[("tc", a)] + e * n_kh + j
                send(piece(buf, s), piece(buf, s), q, q, dev(c_=1 - c))

    def text_finish(a, buf):
        for e in range(n_lx):
            for j in range(n_kh):
                s = tslot(j, (lx + n_lx - e) % n_lx, 1 - c)
                got(piece(buf, s), ids[("tc", a)] + e * n_kh + j)

    def teacher_unit(src, raw, base_id, dst, base):
        raw[l] = src[at(l), :]
        for d in range(1, n_loop):
            got(raw.at[(l + n_loop - d) % n_loop], base_id + d)

        def body(i, _):
            o = pl.multiple_of(i * HALF, HALF)
            xs = [raw[f, pl.ds(o, HALF), :].astype(F32) for f in range(n_loop)]
            x = jnp.concatenate(xs, axis=1)
            _, inv = inv_norm(x)
            dst[pl.ds(pl.multiple_of(base + o, HALF), HALF), :] = (x * inv).astype(BF16)
            return 0
        lax.fori_loop(0, D // HALF, body, 0)

    a2a(ti, raw_i, ids["t_img"])
    a2a(tt, raw_t, ids["t_txt"])
    unit_to(st, own_s, 0)
    text_first(0, own_s, txt_s)
    unit_to(si, img_s, slot0 * D)
    image_first(0, img_s)
    teacher_unit(tt, raw_t, ids["t_txt"], own_t, 0)
    text_first(1, own_t, txt_t)
    teacher_unit(ti, raw_i, ids["t_img"], img_t, slot0 * D)
    image_first(1, img_t)
    image_relay(0, img_s)
    text_relay(0, txt_s)
    text_cross(0, txt_s)
    image_relay(1, img_t)
    text_relay(1, txt_t)
    image_finish(0, img_s)
    text_finish(0, txt_s)

    TILE = 2 * D

    def logits(txt, img, scale, out):
        def body(i, m):
            o = pl.multiple_of(i * TILE, TILE)
            v = scale * lax.dot_general(
                txt[pl.ds(o, TILE), :], img[...], (((1,), (1,)), ((), ())),
                preferred_element_type=F32,
            )
            out[pl.ds(o, TILE), :] = v
            return jnp.maximum(m, jnp.max(v.reshape(TILE // 8, 8, rows), axis=0))
        m = lax.fori_loop(0, cols // TILE, body, jnp.full((8, rows), -jnp.inf, F32))
        return jnp.max(m, axis=0, keepdims=True)

    smax = logits(txt_s, img_s, sscale, slog)
    text_cross(1, txt_t)
    image_finish(1, img_t)
    text_finish(1, txt_t)
    tmax = logits(txt_t, img_t, tscale, tlog)

    def exps(i, carry):
        a, b, x = carry
        o = pl.multiple_of(i * STEP, STEP)
        s = slog[pl.ds(o, STEP), :]
        t = tlog[pl.ds(o, STEP), :]
        es = jnp.exp(s - smax)
        et = jnp.exp(t - tmax)
        slog[pl.ds(o, STEP), :] = es
        tlog[pl.ds(o, STEP), :] = et

        def fold(v):
            return jnp.sum(v.reshape(STEP // 8, 8, rows), axis=0)
        return (a + fold(es), b + fold(et), x + fold(et * (t - s)))

    zero = jnp.zeros((8, rows), F32)
    asum, bsum, xsum = lax.fori_loop(0, cols // STEP, exps, (zero, zero, zero))
    pack = [smax, tmax] + [jnp.sum(v, axis=0, keepdims=True) for v in (asum, bsum, xsum)]
    stat[slot0] = jnp.concatenate(pack + [jnp.zeros((3, rows), F32)], axis=0)
    for d in range(n_kl):
        for e in range(n_ly):
            if d or e:
                q = ids["stat"] + d * n_ly + e
                send(stat.at[slot0], stat.at[slot0], q, q,
                     dev(k_=kh * n_kl + (kl + d) % n_kl, ly_=(ly + e) % n_ly))
    for d in range(n_kl):
        for e in range(n_ly):
            if d or e:
                s = islot((kl + n_kl - d) % n_kl, (ly + n_ly - e) % n_ly)
                got(stat.at[s], ids["stat"] + d * n_ly + e)

    all_stat = [stat[s] for s in range(n_img)]
    gs = functools.reduce(jnp.maximum, [v[0:1] for v in all_stat])
    gt = functools.reduce(jnp.maximum, [v[1:2] for v in all_stat])
    es = [jnp.exp(v[0:1] - gs) for v in all_stat]
    et = [jnp.exp(v[1:2] - gt) for v in all_stat]
    ssum = sum(v[2:3] * e for v, e in zip(all_stat, es))
    tsum = sum(v[3:4] * e for v, e in zip(all_stat, et))
    cross = sum(v[4:5] * e for v, e in zip(all_stat, et))
    diverge = cross / tsum - (gt + jnp.log(tsum)) + (gs + jnp.log(ssum))
    s_mul = sscale * jnp.exp(smax - gs) / ssum
    t_mul = sscale * jnp.exp(tmax - gt) / tsum

    def to_grad(i, _):
        o = pl.multiple_of(i * STEP, STEP)
        v = slog[pl.ds(o, STEP), :] * s_mul - tlog[pl.ds(o, STEP), :] * t_mul
        grad[pl.ds(o, STEP), :] = v.astype(BF16)
        return 0
    lax.fori_loop(0, cols // STEP, to_grad, 0)

    drain()
    for a, own, buf in ((0, own_s, txt_s), (1, own_t, txt_t)):
        text_first_drain(a, own, buf)
    dtxt = txt_t

    def dtxt_pieces(lx_, c_):
        def body(j, _):
            rng = at(tslot(j, lx_, c_))
            dtxt[rng, :] = jnp.dot(grad[rng, :], img_s[...], preferred_element_type=F32).astype(BF16)
            return 0
        lax.fori_loop(0, n_kh, body, 0)

    for e in [*range(1, n_lx), 0]:
        x_ = (lx + e) % n_lx
        dtxt_pieces(x_, 1 - c)
        for j in range(n_kh):
            q = ids["dc"] + e * n_kh + j
            send(piece(dtxt, tslot(j, x_, 1 - c)), r1.at[x_ * n_kh + j], q, q, dev(c_=1 - c))
    for e in range(1, n_lx):
        x_ = (lx + e) % n_lx
        dtxt_pieces(x_, c)
        for j in range(n_kh):
            got(r1.at[x_ * n_kh + j], ids["dc"] + e * n_kh + j)
            rng = at(tslot(j, x_, c))
            dtxt[rng, :] = (dtxt[rng, :].astype(F32) + r1[x_ * n_kh + j].astype(F32)).astype(BF16)
            q = ids["dx"] + e * n_kh + j
            send(piece(dtxt, tslot(j, x_, c)), r2.at[(e - 1) * n_kh + j], q, q, dev(lx_=x_))

    KT = 256
    dimg_acc[...] = jnp.zeros_like(dimg_acc)

    def dimg_body(i, _):
        o = pl.multiple_of(i * KT, KT)
        dimg_acc[...] += lax.dot_general(
            grad[pl.ds(o, KT), :], txt_s[pl.ds(o, KT), :], (((0,), (0,)), ((), ())),
            preferred_element_type=F32,
        )
        return 0
    lax.fori_loop(0, cols // KT, dimg_body, 0)
    dimg = img_t
    for s in range(n_img):
        dimg[pl.ds(s * D, D), :] = dimg_acc[pl.ds(s * D, D), :].astype(BF16)
    for e in range(1, n_ly):
        y_ = (ly + e) % n_ly
        for d in range(n_kl):
            q = ids["gy"] + e * n_kl + d
            send(piece(dimg, islot((kl + d) % n_kl, y_)), ry.at[(e - 1) * n_kl + d], q, q, dev(ly_=y_))

    dtxt_pieces(lx, c)

    for j in range(n_kh):
        got(r1.at[lx * n_kh + j], ids["dc"] + j)
        v = dtxt[at(tslot(j, lx, c)), :].astype(F32) + r1[lx * n_kh + j].astype(F32)
        for e in range(1, n_lx):
            got(r2.at[(e - 1) * n_kh + j], ids["dx"] + e * n_kh + j)
            v = v + r2[(e - 1) * n_kh + j].astype(F32)
        z_rng = at(tslot(j, lx, c))
        dtxt[z_rng, :] = v.astype(BF16)
        dest = kl * n_kh + j
        op = copy(piece(dtxt, tslot(j, lx, c)), r3.at[kh], ids["dz"] + j, ids["dz"] + kh, dev(k_=dest))

        @pl.when(dest != k)
        def _():
            op.start()

        @pl.when(dest == k)
        def _():
            r3[kh] = dtxt[z_rng, :]

    def image_sum(d):
        v = dimg[at(islot((kl + d) % n_kl, ly)), :].astype(F32)
        for e in range(1, n_ly):
            v = v + ry[(e - 1) * n_kl + d].astype(F32)
        return v

    for e in range(1, n_ly):
        for d in range(n_kl):
            got(ry.at[(e - 1) * n_kl + d], ids["gy"] + e * n_kl + d)
    for d in range(1, n_kl):
        pair_slot = islot((kl + d) % n_kl, ly)
        dimg[at(pair_slot), :] = image_sum(d).astype(BF16)
        q = ids["gz"] + d
        send(piece(dimg, pair_slot), rz.at[d - 1], q, q, dev(k_=kh * n_kl + (kl + d) % n_kl))

    total = jnp.broadcast_to(jnp.sum(diverge, axis=1, keepdims=True), (8, 128))
    part[kh] = total
    for d in range(1, n_kh):
        q = ids["lk"] + d
        send(part.at[kh], part.at[kh], q, q, dev(k_=((kh + d) % n_kh) * n_kl + kl))
    for d in range(1, n_kh):
        got(part.at[(kh + n_kh - d) % n_kh], ids["lk"] + d)
    base = n_kh
    total = sum(part[i] for i in range(n_kh))
    part[base + lx] = total
    for d in range(1, n_lx):
        q = ids["lx"] + d
        send(part.at[base + lx], part.at[base + lx], q, q, dev(lx_=(lx + d) % n_lx))
    for d in range(1, n_lx):
        got(part.at[base + (lx + n_lx - d) % n_lx], ids["lx"] + d)
    total = sum(part[base + i] for i in range(n_lx))
    base = n_kh + n_lx
    part[base + c] = total
    send(part.at[base + c], part.at[base + c], ids["lc"], ids["lc"], dev(c_=1 - c))
    got(part.at[base + 1 - c], ids["lc"])
    total = part[base] + part[base + 1]
    loss_out[...] = total / float(D * n_row * n_loop)

    def finish(src, terms, out):
        def body(i, _):
            rng = pl.ds(pl.multiple_of(i * HALF, HALF), HALF)
            x = src[rng, :].astype(F32)
            n, inv = inv_norm(x)
            u = x * inv
            g = terms(rng)
            inner = jnp.sum(g * u, axis=1, keepdims=True)
            out[rng, :] = ((g - u * inner) * inv).astype(BF16)
            return 0
        lax.fori_loop(0, D // HALF, body, 0)

    for d in range(1, n_kl):
        got(rz.at[d - 1], ids["gz"] + d)

    def image_terms(rng):
        o = pl.multiple_of(slot0 * D + rng.start, HALF)
        v = dimg[pl.ds(o, HALF), :].astype(F32)
        for e in range(1, n_ly):
            v = v + ry[(e - 1) * n_kl, rng, :].astype(F32)
        for d in range(1, n_kl):
            v = v + rz[d - 1, rng, :].astype(F32)
        return v
    finish(si, image_terms, gi_out)

    for h in range(n_kh):
        @pl.when(h * n_kl + src_kl != k)
        def _():
            got(r3.at[h], ids["dz"] + h)
    finish(st, lambda rng: sum(r3[h, rng, :].astype(F32) for h in range(n_kh)), gt_out)

    drain()
    for j in range(n_kh):
        dest = kl * n_kh + j
        op = copy(piece(dtxt, tslot(j, lx, c)), r3.at[kh], ids["dz"] + j, ids["dz"] + kh, dev(k_=dest))

        @pl.when(dest != k)
        def _():
            op.wait_send()


def on_device(n_row, n_loop, si, st, ti, tt, ssc, tsc):
    D, code = si.shape
    n_kl, n_lx = 2, 2
    n_kh, n_ly = n_row // (2 * n_kl), n_loop // n_lx
    n_img, n_txt = n_kl * n_ly, n_kh * n_lx * 2
    rows, cols = n_img * D, n_txt * D
    ids = make_ids(n_loop, n_kh, n_kl, n_lx, n_ly)
    dims = (n_row, n_loop, n_kh, n_kl, n_lx, n_ly, D, code)
    vm = pl.BlockSpec(memory_space=pltpu.VMEM)
    sm = pl.BlockSpec(memory_space=pltpu.SMEM)
    V = pltpu.VMEM
    loss, gi, gt = pl.pallas_call(
        functools.partial(kernel, dims, ids),
        out_shape=(
            jax.ShapeDtypeStruct((8, 128), F32),
            jax.ShapeDtypeStruct((D, code), BF16),
            jax.ShapeDtypeStruct((D, code), BF16),
        ),
        in_specs=[vm] * 4 + [sm] * 2,
        out_specs=(vm, vm, vm),
        scratch_shapes=[
            V((rows, code), BF16), V((rows, code), BF16),
            V((D, code), BF16), V((D, code), BF16),
            V((cols, code), BF16), V((cols, code), BF16),
            V((n_loop, D, code // n_loop), BF16), V((n_loop, D, code // n_loop), BF16),
            V((cols, rows), F32), V((cols, rows), F32), V((cols, rows), BF16),
            V((n_img, 8, rows), F32),
            V((rows, code), F32),
            V((n_lx * n_kh, D, code), BF16),
            V(((n_lx - 1) * n_kh, D, code), BF16),
            V((n_kh, D, code), BF16),
            V(((n_ly - 1) * n_kl, D, code), BF16),
            V((n_kl - 1, D, code), BF16),
            V((n_kh + n_lx + 2, 8, 128), F32),
            pltpu.SemaphoreType.DMA((ids.count,)),
            pltpu.SemaphoreType.DMA((ids.count,)),
        ],
        compiler_params=pltpu.CompilerParams(
            collective_id=0, has_side_effects=True, vmem_limit_bytes=67043328,
        ),
    )(si, st, ti, tt, ssc, tsc)
    return loss[0, :1], gi, gt


def solution(mesh):
    return jax.shard_map(
        functools.partial(on_device, mesh.shape["row"], mesh.shape["loop"]),
        mesh=mesh,
        in_specs=(
            P(("row", "loop"), None),
            P(("row", "loop"), None),
            P("row", "loop"),
            P("row", "loop"),
            P(),
            P(),
        ),
        out_specs=(P(), P(("row", "loop"), None), P(("row", "loop"), None)),
        check_vma=False,
    )
```

```python
import functools
import jax
import jax.numpy as jnp
from jax import lax
from jax.experimental import pallas as pl
from jax.experimental.pallas import tpu as pltpu
from jax.sharding import PartitionSpec as P

EPS = 1e-06
F32 = jnp.float32
BF16 = jnp.bfloat16
MESH = pl.DeviceIdType.MESH
STEP = 32
CHUNKS = 2


class Ids:
    def __init__(self):
        self.table = {}
        self.count = 0

    def take(self, name, size=1):
        self.table[name] = self.count
        self.count += size

    def __getitem__(self, name):
        return self.table[name]


def make_ids(n_loop, n_kh, n_kl, n_lx, n_ly):
    ids = Ids()
    ids.take("t_img", n_loop)
    ids.take("t_txt", n_loop)
    for a in range(2):
        ids.take(("iz", a), n_kl * CHUNKS)
        ids.take(("iy", a), n_ly * n_kl * CHUNKS)
        ids.take(("tz", a), n_kh * CHUNKS)
        ids.take(("tx", a), n_lx * n_kh * CHUNKS)
        ids.take(("tc", a), n_lx * n_kh * CHUNKS)
    ids.take("stat", n_kl * n_ly)
    ids.take("dc", n_lx * n_kh * CHUNKS)
    ids.take("dx", n_lx * n_kh * CHUNKS)
    ids.take("dz", n_kh * CHUNKS)
    ids.take("gy", n_ly * n_kl * CHUNKS)
    ids.take("gz", n_kl * CHUNKS)
    ids.take("lk", n_kh)
    ids.take("lx", n_lx)
    ids.take("lc", 1)
    return ids


def kernel(
    dims, ids,
    si, st, ti, tt, ssc, tsc,
    loss_out, gi_out, gt_out,
    img_s, img_t, own_s, own_t, txt_s, txt_t, raw_i, raw_t,
    slog, tlog, grad, stat, dimg_acc, r1, r2, r3, ry, rz, part,
    ss, rs,
):
    n_row, n_loop, n_kh, n_kl, n_lx, n_ly, D, code = dims
    n_img = n_kl * n_ly
    n_txt = n_kh * n_lx * 2
    rows = n_img * D
    Dc = D // CHUNKS
    cols = n_txt * D
    feat = code // n_loop
    r = lax.axis_index("row")
    l = lax.axis_index("loop")
    k, c = r // 2, r % 2
    kh, kl = k // n_kl, k % n_kl
    src_kl, src_j = k // n_kh, k % n_kh
    ly, lx = l // n_lx, l % n_lx
    sscale = ssc[0]
    tscale = tsc[0]

    def dev(k_=None, c_=None, ly_=None, lx_=None):
        kk = k if k_ is None else k_
        cc = c if c_ is None else c_
        yy = ly if ly_ is None else ly_
        xx = lx if lx_ is None else lx_
        return (kk * 2 + cc, yy * n_lx + xx)

    def piece(ref, slot):
        return ref.at[pl.ds(pl.multiple_of(slot * D, D), D), :]

    def chunk(ref, slot, h):
        return ref.at[pl.ds(pl.multiple_of(slot * D + h * Dc, Dc), Dc), :]

    def chunk_of(ref, i, h):
        return ref.at[i, pl.ds(h * Dc, Dc), :]

    def at(slot):
        return pl.ds(pl.multiple_of(slot * D, D), D)

    def copy(src, dst, q_send, q_recv, device):
        return pltpu.make_async_remote_copy(
            src_ref=src, dst_ref=dst, send_sem=ss.at[q_send], recv_sem=rs.at[q_recv],
            device_id=device, device_id_type=MESH,
        )

    sent = []

    def send(src, dst, q_send, q_recv, device):
        op = copy(src, dst, q_send, q_recv, device)
        op.start()
        sent.append(op)

    def got(dst, q):
        copy(dst, dst, q, q, dev(c_=1 - c)).wait_recv()

    def drain():
        for op in sent:
            op.wait_send()
        sent.clear()

    barrier = pltpu.get_barrier_semaphore()
    n_peer = 0
    for d in range(1, n_loop):
        pl.semaphore_signal(barrier, inc=1, device_id=(r, (l + d) % n_loop), device_id_type=MESH)
        n_peer += 1
    for d in range(1, n_kh * n_kl):
        pl.semaphore_signal(barrier, inc=1, device_id=dev(k_=(k + d) % (n_kh * n_kl)), device_id_type=MESH)
        n_peer += 1
    pl.semaphore_signal(barrier, inc=1, device_id=dev(c_=1 - c), device_id_type=MESH)
    n_peer += 1
    for d in range(1, n_kl):
        for e in range(1, n_ly):
            diagonal = dev(k_=kh * n_kl + (kl + d) % n_kl, ly_=(ly + e) % n_ly)
            pl.semaphore_signal(barrier, inc=1, device_id=diagonal, device_id_type=MESH)
            n_peer += 1
    pl.semaphore_wait(barrier, n_peer)

    slot0 = kl * n_ly + ly

    def islot(kl_, ly_):
        return kl_ * n_ly + ly_

    def tslot(j, lx_, c_):
        return (j * n_lx + lx_) * 2 + c_

    def inv_norm(x):
        n2 = jnp.sum(x * x, axis=1, keepdims=True) + EPS
        n = jnp.sqrt(n2)
        return n, 1.0 / n

    HALF = 16

    def unit_to(src, dst, base, h):
        def body(i, _):
            o = pl.multiple_of(h * Dc + i * HALF, HALF)
            x = src[pl.ds(o, HALF), :].astype(F32)
            _, inv = inv_norm(x)
            dst[pl.ds(pl.multiple_of(base + o, HALF), HALF), :] = (x * inv).astype(BF16)
            return 0
        lax.fori_loop(0, Dc // HALF, body, 0)

    def a2a(src, raw, base):
        for d in range(1, n_loop):
            peer = (l + d) % n_loop
            send(piece(src, peer), raw.at[l], base + d, base + d, (r, peer))

    def image_first(a, buf, h):
        for d in range(1, n_kl):
            p = (kl + d) % n_kl
            q = ids[("iz", a)] + d * CHUNKS + h
            send(chunk(buf, slot0, h), chunk(buf, slot0, h), q, q, dev(k_=kh * n_kl + p))
        for e in range(1, n_ly):
            q = ids[("iy", a)] + e * n_kl * CHUNKS + h
            send(chunk(buf, slot0, h), chunk(buf, slot0, h), q, q, dev(ly_=(ly + e) % n_ly))

    def image_relay(a, buf, h):
        for d in range(1, n_kl):
            s = islot((kl + n_kl - d) % n_kl, ly)
            got(chunk(buf, s, h), ids[("iz", a)] + d * CHUNKS + h)
            for e in range(1, n_ly):
                q = ids[("iy", a)] + (e * n_kl + d) * CHUNKS + h
                send(chunk(buf, s, h), chunk(buf, s, h), q, q, dev(ly_=(ly + e) % n_ly))

    def image_finish(a, buf):
        for h in range(CHUNKS):
            for e in range(1, n_ly):
                for d in range(n_kl):
                    s = islot((kl + n_kl - d) % n_kl, (ly + n_ly - e) % n_ly)
                    got(chunk(buf, s, h), ids[("iy", a)] + (e * n_kl + d) * CHUNKS + h)

    def text_first_copy(a, own, buf, h, g):
        dest = g * n_kl + src_kl
        q = ids[("tz", a)]
        s = tslot(src_j, lx, c)
        op = copy(chunk(own, 0, h), chunk(buf, s, h), q + g * CHUNKS + h,
                  q + src_j * CHUNKS + h, dev(k_=dest))
        return dest, op

    def text_first(a, own, buf, h):
        for g in range(n_kh):
            dest, op = text_first_copy(a, own, buf, h, g)

            @pl.when(dest != k)
            def _():
                op.start()

            @pl.when(dest == k)
            def _():
                o = pl.multiple_of(tslot(src_j, lx, c) * D + h * Dc, Dc)
                buf[pl.ds(o, Dc), :] = own[pl.ds(h * Dc, Dc), :]

    def text_first_drain(a, own, buf):
        for h in range(CHUNKS):
            for g in range(n_kh):
                dest, op = text_first_copy(a, own, buf, h, g)

                @pl.when(dest != k)
                def _():
                    op.wait_send()

    def text_relay(a, buf, h):
        for j in range(n_kh):
            s = tslot(j, lx, c)

            @pl.when(kl * n_kh + j != k)
            def _():
                got(chunk(buf, s, h), ids[("tz", a)] + j * CHUNKS + h)

            for e in range(1, n_lx):
                q = ids[("tx", a)] + (e * n_kh + j) * CHUNKS + h
                send(chunk(buf, s, h), chunk(buf, s, h), q, q, dev(lx_=(lx + e) % n_lx))
            q = ids[("tc", a)] + j * CHUNKS + h
            send(chunk(buf, s, h), chunk(buf, s, h), q, q, dev(c_=1 - c))

    def text_cross(a, buf, h):
        for e in range(1, n_lx):
            for j in range(n_kh):
                s = tslot(j, (lx + n_lx - e) % n_lx, c)
                got(chunk(buf, s, h), ids[("tx", a)] + (e * n_kh + j) * CHUNKS + h)
                q = ids[("tc", a)] + (e * n_kh + j) * CHUNKS + h
                send(chunk(buf, s, h), chunk(buf, s, h), q, q, dev(c_=1 - c))

    def text_finish(a, buf):
        for h in range(CHUNKS):
            for e in range(n_lx):
                for j in range(n_kh):
                    s = tslot(j, (lx + n_lx - e) % n_lx, 1 - c)
                    got(chunk(buf, s, h), ids[("tc", a)] + (e * n_kh + j) * CHUNKS + h)

    def teacher_wait(src, raw, base_id):
        raw[l] = src[at(l), :]
        for d in range(1, n_loop):
            got(raw.at[(l + n_loop - d) % n_loop], base_id + d)

    def teacher_unit(raw, dst, base, h):
        def body(i, _):
            o = pl.multiple_of(h * Dc + i * HALF, HALF)
            xs = [raw[f, pl.ds(o, HALF), :].astype(F32) for f in range(n_loop)]
            x = jnp.concatenate(xs, axis=1)
            _, inv = inv_norm(x)
            dst[pl.ds(pl.multiple_of(base + o, HALF), HALF), :] = (x * inv).astype(BF16)
            return 0
        lax.fori_loop(0, Dc // HALF, body, 0)

    a2a(tt, raw_t, ids["t_txt"])
    a2a(ti, raw_i, ids["t_img"])
    for h in range(CHUNKS):
        unit_to(st, own_s, 0, h)
        text_first(0, own_s, txt_s, h)
        unit_to(si, img_s, slot0 * D, h)
        image_first(0, img_s, h)
    for h in range(CHUNKS):
        text_relay(0, txt_s, h)
        image_relay(0, img_s, h)
        if h == 0:
            teacher_wait(tt, raw_t, ids["t_txt"])
        teacher_unit(raw_t, own_t, 0, h)
        text_first(1, own_t, txt_t, h)
        if h == 0:
            teacher_wait(ti, raw_i, ids["t_img"])
        teacher_unit(raw_i, img_t, slot0 * D, h)
        image_first(1, img_t, h)
    for h in range(CHUNKS):
        text_cross(0, txt_s, h)
        text_relay(1, txt_t, h)
        image_relay(1, img_t, h)
    image_finish(0, img_s)
    text_finish(0, txt_s)

    TILE = 2 * D

    def logits(txt, img, scale, out):
        def body(i, m):
            o = pl.multiple_of(i * TILE, TILE)
            v = scale * lax.dot_general(
                txt[pl.ds(o, TILE), :], img[...], (((1,), (1,)), ((), ())),
                preferred_element_type=F32,
            )
            out[pl.ds(o, TILE), :] = v
            return jnp.maximum(m, jnp.max(v.reshape(TILE // 8, 8, rows), axis=0))
        m = lax.fori_loop(0, cols // TILE, body, jnp.full((8, rows), -jnp.inf, F32))
        return jnp.max(m, axis=0, keepdims=True)

    smax = logits(txt_s, img_s, sscale, slog)
    for h in range(CHUNKS):
        text_cross(1, txt_t, h)
    image_finish(1, img_t)
    text_finish(1, txt_t)
    tmax = logits(txt_t, img_t, tscale, tlog)

    def exps(i, carry):
        a, b, x = carry
        o = pl.multiple_of(i * STEP, STEP)
        s = slog[pl.ds(o, STEP), :]
        t = tlog[pl.ds(o, STEP), :]
        es = jnp.exp(s - smax)
        et = jnp.exp(t - tmax)
        slog[pl.ds(o, STEP), :] = es
        tlog[pl.ds(o, STEP), :] = et

        def fold(v):
            return jnp.sum(v.reshape(STEP // 8, 8, rows), axis=0)
        return (a + fold(es), b + fold(et), x + fold(et * (t - s)))

    zero = jnp.zeros((8, rows), F32)
    asum, bsum, xsum = lax.fori_loop(0, cols // STEP, exps, (zero, zero, zero))
    pack = [smax, tmax] + [jnp.sum(v, axis=0, keepdims=True) for v in (asum, bsum, xsum)]
    stat[slot0] = jnp.concatenate(pack + [jnp.zeros((3, rows), F32)], axis=0)
    for d in range(n_kl):
        for e in range(n_ly):
            if d or e:
                q = ids["stat"] + d * n_ly + e
                send(stat.at[slot0], stat.at[slot0], q, q,
                     dev(k_=kh * n_kl + (kl + d) % n_kl, ly_=(ly + e) % n_ly))
    for d in range(n_kl):
        for e in range(n_ly):
            if d or e:
                s = islot((kl + n_kl - d) % n_kl, (ly + n_ly - e) % n_ly)
                got(stat.at[s], ids["stat"] + d * n_ly + e)

    all_stat = [stat[s] for s in range(n_img)]
    gs = functools.reduce(jnp.maximum, [v[0:1] for v in all_stat])
    gt = functools.reduce(jnp.maximum, [v[1:2] for v in all_stat])
    es = [jnp.exp(v[0:1] - gs) for v in all_stat]
    et = [jnp.exp(v[1:2] - gt) for v in all_stat]
    ssum = sum(v[2:3] * e for v, e in zip(all_stat, es))
    tsum = sum(v[3:4] * e for v, e in zip(all_stat, et))
    cross = sum(v[4:5] * e for v, e in zip(all_stat, et))
    diverge = cross / tsum - (gt + jnp.log(tsum)) + (gs + jnp.log(ssum))
    s_mul = sscale * jnp.exp(smax - gs) / ssum
    t_mul = sscale * jnp.exp(tmax - gt) / tsum

    def to_grad(i, _):
        o = pl.multiple_of(i * STEP, STEP)
        v = slog[pl.ds(o, STEP), :] * s_mul - tlog[pl.ds(o, STEP), :] * t_mul
        grad[pl.ds(o, STEP), :] = v.astype(BF16)
        return 0
    lax.fori_loop(0, cols // STEP, to_grad, 0)

    drain()
    for a, own, buf in ((0, own_s, txt_s), (1, own_t, txt_t)):
        text_first_drain(a, own, buf)
    dtxt = txt_t

    def dtxt_pieces(lx_, c_):
        def body(j, _):
            rng = at(tslot(j, lx_, c_))
            dtxt[rng, :] = jnp.dot(grad[rng, :], img_s[...], preferred_element_type=F32).astype(BF16)
            return 0
        lax.fori_loop(0, n_kh, body, 0)

    def to_core(e):
        x_ = (lx + e) % n_lx
        dtxt_pieces(x_, 1 - c)
        for h in range(CHUNKS):
            for j in range(n_kh):
                q = ids["dc"] + (e * n_kh + j) * CHUNKS + h
                send(chunk(dtxt, tslot(j, x_, 1 - c), h), chunk_of(r1, x_ * n_kh + j, h), q, q, dev(c_=1 - c))

    def chunk_rows(slot, h):
        return pl.ds(pl.multiple_of(slot * D + h * Dc, Dc), Dc)

    half = [pl.ds(h * Dc, Dc) for h in range(CHUNKS)]

    for e in range(1, n_lx):
        x_ = (lx + e) % n_lx
        to_core(e)
        dtxt_pieces(x_, c)
        for h in range(CHUNKS):
            for j in range(n_kh):
                i = x_ * n_kh + j
                got(chunk_of(r1, i, h), ids["dc"] + (e * n_kh + j) * CHUNKS + h)
                rng = chunk_rows(tslot(j, x_, c), h)
                dtxt[rng, :] = (dtxt[rng, :].astype(F32) + r1[i, half[h], :].astype(F32)).astype(BF16)
                q = ids["dx"] + (e * n_kh + j) * CHUNKS + h
                send(chunk(dtxt, tslot(j, x_, c), h), chunk_of(r2, (e - 1) * n_kh + j, h), q, q, dev(lx_=x_))

    KT = 256
    dimg_acc[...] = jnp.zeros_like(dimg_acc)

    def dimg_body(i, _):
        o = pl.multiple_of(i * KT, KT)
        dimg_acc[...] += lax.dot_general(
            grad[pl.ds(o, KT), :], txt_s[pl.ds(o, KT), :], (((0,), (0,)), ((), ())),
            preferred_element_type=F32,
        )
        return 0
    lax.fori_loop(0, cols // KT, dimg_body, 0)
    dimg = img_t
    for s in range(n_img):
        dimg[pl.ds(s * D, D), :] = dimg_acc[pl.ds(s * D, D), :].astype(BF16)
    for d in [*range(1, n_kl), 0]:
        for h in range(CHUNKS):
            for e in range(1, n_ly):
                y_ = (ly + e) % n_ly
                q = ids["gy"] + (e * n_kl + d) * CHUNKS + h
                send(chunk(dimg, islot((kl + d) % n_kl, y_), h), chunk_of(ry, (e - 1) * n_kl + d, h), q, q, dev(ly_=y_))

    to_core(0)
    dtxt_pieces(lx, c)

    def owner_copy(j, h):
        dest = kl * n_kh + j
        op = copy(chunk(dtxt, tslot(j, lx, c), h), chunk_of(r3, kh, h),
                  ids["dz"] + j * CHUNKS + h, ids["dz"] + kh * CHUNKS + h, dev(k_=dest))
        return dest, op

    def text_sum(j, h):
        got(chunk_of(r1, lx * n_kh + j, h), ids["dc"] + j * CHUNKS + h)
        rng = chunk_rows(tslot(j, lx, c), h)
        v = dtxt[rng, :].astype(F32) + r1[lx * n_kh + j, half[h], :].astype(F32)
        for e in range(1, n_lx):
            got(chunk_of(r2, (e - 1) * n_kh + j, h), ids["dx"] + (e * n_kh + j) * CHUNKS + h)
            v = v + r2[(e - 1) * n_kh + j, half[h], :].astype(F32)
        dtxt[rng, :] = v.astype(BF16)
        dest, op = owner_copy(j, h)

        @pl.when(dest != k)
        def _():
            op.start()

        @pl.when(dest == k)
        def _():
            r3[kh, half[h], :] = dtxt[rng, :]

    def got_y(d, h):
        for e in range(1, n_ly):
            got(chunk_of(ry, (e - 1) * n_kl + d, h), ids["gy"] + (e * n_kl + d) * CHUNKS + h)

    def image_sum(d, h):
        got_y(d, h)
        pair_slot = islot((kl + d) % n_kl, ly)
        rng = chunk_rows(pair_slot, h)
        v = dimg[rng, :].astype(F32)
        for e in range(1, n_ly):
            v = v + ry[(e - 1) * n_kl + d, half[h], :].astype(F32)
        dimg[rng, :] = v.astype(BF16)
        q = ids["gz"] + d * CHUNKS + h
        send(chunk(dimg, pair_slot, h), chunk_of(rz, d - 1, h), q, q, dev(k_=kh * n_kl + (kl + d) % n_kl))

    for h in range(CHUNKS):
        for j in range(n_kh):
            text_sum(j, h)
        for d in range(1, n_kl):
            image_sum(d, h)
    for h in range(CHUNKS):
        got_y(0, h)

    total = jnp.broadcast_to(jnp.sum(diverge, axis=1, keepdims=True), (8, 128))
    part[kh] = total
    for d in range(1, n_kh):
        q = ids["lk"] + d
        send(part.at[kh], part.at[kh], q, q, dev(k_=((kh + d) % n_kh) * n_kl + kl))
    for d in range(1, n_kh):
        got(part.at[(kh + n_kh - d) % n_kh], ids["lk"] + d)
    base = n_kh
    total = sum(part[i] for i in range(n_kh))
    part[base + lx] = total
    for d in range(1, n_lx):
        q = ids["lx"] + d
        send(part.at[base + lx], part.at[base + lx], q, q, dev(lx_=(lx + d) % n_lx))
    for d in range(1, n_lx):
        got(part.at[base + (lx + n_lx - d) % n_lx], ids["lx"] + d)
    total = sum(part[base + i] for i in range(n_lx))
    base = n_kh + n_lx
    part[base + c] = total
    send(part.at[base + c], part.at[base + c], ids["lc"], ids["lc"], dev(c_=1 - c))
    got(part.at[base + 1 - c], ids["lc"])
    total = part[base] + part[base + 1]
    loss_out[...] = total / float(D * n_row * n_loop)

    def finish(src, terms, out):
        def body(i, _):
            rng = pl.ds(pl.multiple_of(i * HALF, HALF), HALF)
            x = src[rng, :].astype(F32)
            n, inv = inv_norm(x)
            u = x * inv
            g = terms(rng)
            inner = jnp.sum(g * u, axis=1, keepdims=True)
            out[rng, :] = ((g - u * inner) * inv).astype(BF16)
            return 0
        lax.fori_loop(0, D // HALF, body, 0)

    for d in range(1, n_kl):
        for h in range(CHUNKS):
            got(chunk_of(rz, d - 1, h), ids["gz"] + d * CHUNKS + h)

    def image_terms(rng):
        o = pl.multiple_of(slot0 * D + rng.start, HALF)
        v = dimg[pl.ds(o, HALF), :].astype(F32)
        for e in range(1, n_ly):
            v = v + ry[(e - 1) * n_kl, rng, :].astype(F32)
        for d in range(1, n_kl):
            v = v + rz[d - 1, rng, :].astype(F32)
        return v
    finish(si, image_terms, gi_out)

    for g in range(n_kh):
        @pl.when(g * n_kl + src_kl != k)
        def _():
            for h in range(CHUNKS):
                got(chunk_of(r3, g, h), ids["dz"] + g * CHUNKS + h)
    finish(st, lambda rng: sum(r3[g, rng, :].astype(F32) for g in range(n_kh)), gt_out)

    drain()
    for j in range(n_kh):
        for h in range(CHUNKS):
            dest, op = owner_copy(j, h)

            @pl.when(dest != k)
            def _():
                op.wait_send()


def on_device(n_row, n_loop, si, st, ti, tt, ssc, tsc):
    D, code = si.shape
    n_kl, n_lx = 2, 2
    n_kh, n_ly = n_row // (2 * n_kl), n_loop // n_lx
    n_img, n_txt = n_kl * n_ly, n_kh * n_lx * 2
    rows, cols = n_img * D, n_txt * D
    ids = make_ids(n_loop, n_kh, n_kl, n_lx, n_ly)
    dims = (n_row, n_loop, n_kh, n_kl, n_lx, n_ly, D, code)
    vm = pl.BlockSpec(memory_space=pltpu.VMEM)
    sm = pl.BlockSpec(memory_space=pltpu.SMEM)
    V = pltpu.VMEM
    loss, gi, gt = pl.pallas_call(
        functools.partial(kernel, dims, ids),
        out_shape=(
            jax.ShapeDtypeStruct((8, 128), F32),
            jax.ShapeDtypeStruct((D, code), BF16),
            jax.ShapeDtypeStruct((D, code), BF16),
        ),
        in_specs=[vm] * 4 + [sm] * 2,
        out_specs=(vm, vm, vm),
        scratch_shapes=[
            V((rows, code), BF16), V((rows, code), BF16),
            V((D, code), BF16), V((D, code), BF16),
            V((cols, code), BF16), V((cols, code), BF16),
            V((n_loop, D, code // n_loop), BF16), V((n_loop, D, code // n_loop), BF16),
            V((cols, rows), F32), V((cols, rows), F32), V((cols, rows), BF16),
            V((n_img, 8, rows), F32),
            V((rows, code), F32),
            V((n_lx * n_kh, D, code), BF16),
            V(((n_lx - 1) * n_kh, D, code), BF16),
            V((n_kh, D, code), BF16),
            V(((n_ly - 1) * n_kl, D, code), BF16),
            V((n_kl - 1, D, code), BF16),
            V((n_kh + n_lx + 2, 8, 128), F32),
            pltpu.SemaphoreType.DMA((ids.count,)),
            pltpu.SemaphoreType.DMA((ids.count,)),
        ],
        compiler_params=pltpu.CompilerParams(
            collective_id=0, has_side_effects=True, vmem_limit_bytes=67043328,
        ),
    )(si, st, ti, tt, ssc, tsc)
    return loss[0, :1], gi, gt


def solution(mesh):
    return jax.shard_map(
        functools.partial(on_device, mesh.shape["row"], mesh.shape["loop"]),
        mesh=mesh,
        in_specs=(
            P(("row", "loop"), None),
            P(("row", "loop"), None),
            P("row", "loop"),
            P("row", "loop"),
            P(),
            P(),
        ),
        out_specs=(P(), P(("row", "loop"), None), P(("row", "loop"), None)),
        check_vma=False,
    )
```

```python
import functools
import jax
import jax.numpy as jnp
from jax import lax
from jax.experimental import pallas as pl
from jax.experimental.pallas import tpu as pltpu
from jax.sharding import PartitionSpec as P

EPS = 1e-06
F32 = jnp.float32
BF16 = jnp.bfloat16
MESH = pl.DeviceIdType.MESH
STEP = 32
CHUNKS = 2


class Ids:
    def __init__(self):
        self.table = {}
        self.count = 0

    def take(self, name, size=1):
        self.table[name] = self.count
        self.count += size

    def __getitem__(self, name):
        return self.table[name]


def make_ids(n_loop, n_kh, n_kl, n_lx, n_ly):
    ids = Ids()
    ids.take("t_img", n_loop)
    ids.take("t_txt", n_loop)
    for a in range(2):
        ids.take(("iz", a), n_kl * CHUNKS)
        ids.take(("iy", a), n_ly * n_kl * CHUNKS)
        ids.take(("tz", a), n_kh * CHUNKS)
        ids.take(("tx", a), n_lx * n_kh * CHUNKS)
        ids.take(("tc", a), n_lx * n_kh * CHUNKS)
    ids.take("stat", n_kl * n_ly)
    ids.take("dc", n_lx * n_kh * CHUNKS)
    ids.take("dx", n_lx * n_kh * CHUNKS)
    ids.take("dz", n_kh * CHUNKS)
    ids.take("gy", n_ly * n_kl * CHUNKS)
    ids.take("gz", n_kl * CHUNKS)
    ids.take("lk", n_kh)
    ids.take("lx", n_lx)
    ids.take("lc", 1)
    return ids


def kernel(
    dims, ids,
    si, st, ti, tt, ssc, tsc,
    loss_out, gi_out, gt_out,
    img_s, img_t, own_s, own_t, txt_s, txt_t, raw_i, raw_t,
    slog, tlog, grad, stat, dimg_acc, r1, r2, r3, ry, rz, part,
    ss, rs,
):
    n_row, n_loop, n_kh, n_kl, n_lx, n_ly, D, code = dims
    n_img = n_kl * n_ly
    n_txt = n_kh * n_lx * 2
    rows = n_img * D
    Dc = D // CHUNKS
    cols = n_txt * D
    feat = code // n_loop
    r = lax.axis_index("row")
    l = lax.axis_index("loop")
    k, c = r // 2, r % 2
    kh, kl = k // n_kl, k % n_kl
    src_kl, src_j = k // n_kh, k % n_kh
    ly, lx = l // n_lx, l % n_lx
    sscale = ssc[0]
    tscale = tsc[0]

    def dev(k_=None, c_=None, ly_=None, lx_=None):
        kk = k if k_ is None else k_
        cc = c if c_ is None else c_
        yy = ly if ly_ is None else ly_
        xx = lx if lx_ is None else lx_
        return (kk * 2 + cc, yy * n_lx + xx)

    def piece(ref, slot):
        return ref.at[pl.ds(pl.multiple_of(slot * D, D), D), :]

    def chunk(ref, slot, h):
        return ref.at[pl.ds(pl.multiple_of(slot * D + h * Dc, Dc), Dc), :]

    def chunk_of(ref, i, h):
        return ref.at[i, pl.ds(h * Dc, Dc), :]

    def at(slot):
        return pl.ds(pl.multiple_of(slot * D, D), D)

    def copy(src, dst, q_send, q_recv, device):
        return pltpu.make_async_remote_copy(
            src_ref=src, dst_ref=dst, send_sem=ss.at[q_send], recv_sem=rs.at[q_recv],
            device_id=device, device_id_type=MESH,
        )

    sent = []

    def send(src, dst, q_send, q_recv, device):
        op = copy(src, dst, q_send, q_recv, device)
        op.start()
        sent.append(op)

    def got(dst, q):
        copy(dst, dst, q, q, dev(c_=1 - c)).wait_recv()

    def drain():
        for op in sent:
            op.wait_send()
        sent.clear()

    barrier = pltpu.get_barrier_semaphore()
    n_peer = 0
    for d in range(1, n_loop):
        pl.semaphore_signal(barrier, inc=1, device_id=(r, (l + d) % n_loop), device_id_type=MESH)
        n_peer += 1
    for d in range(1, n_kh * n_kl):
        pl.semaphore_signal(barrier, inc=1, device_id=dev(k_=(k + d) % (n_kh * n_kl)), device_id_type=MESH)
        n_peer += 1
    pl.semaphore_signal(barrier, inc=1, device_id=dev(c_=1 - c), device_id_type=MESH)
    n_peer += 1
    for d in range(1, n_kl):
        for e in range(1, n_ly):
            diagonal = dev(k_=kh * n_kl + (kl + d) % n_kl, ly_=(ly + e) % n_ly)
            pl.semaphore_signal(barrier, inc=1, device_id=diagonal, device_id_type=MESH)
            n_peer += 1
    pl.semaphore_wait(barrier, n_peer)

    slot0 = kl * n_ly + ly

    def islot(kl_, ly_):
        return kl_ * n_ly + ly_

    def tslot(j, lx_, c_):
        return (j * n_lx + lx_) * 2 + c_

    def inv_norm(x):
        n2 = jnp.sum(x * x, axis=1, keepdims=True) + EPS
        n = jnp.sqrt(n2)
        return n, 1.0 / n

    HALF = Dc if Dc <= 80 else 16

    def unit_to(src, dst, base, h):
        def body(i, _):
            o = pl.multiple_of(h * Dc + i * HALF, HALF)
            x = src[pl.ds(o, HALF), :].astype(F32)
            _, inv = inv_norm(x)
            dst[pl.ds(pl.multiple_of(base + o, HALF), HALF), :] = (x * inv).astype(BF16)
            return 0
        lax.fori_loop(0, Dc // HALF, body, 0)

    def a2a(src, raw, base):
        for d in range(1, n_loop):
            peer = (l + d) % n_loop
            send(piece(src, peer), raw.at[l], base + d, base + d, (r, peer))

    def image_first(a, buf, h):
        for d in range(1, n_kl):
            p = (kl + d) % n_kl
            q = ids[("iz", a)] + d * CHUNKS + h
            send(chunk(buf, slot0, h), chunk(buf, slot0, h), q, q, dev(k_=kh * n_kl + p))
        for e in range(1, n_ly):
            q = ids[("iy", a)] + e * n_kl * CHUNKS + h
            send(chunk(buf, slot0, h), chunk(buf, slot0, h), q, q, dev(ly_=(ly + e) % n_ly))

    def image_relay(a, buf, h):
        for d in range(1, n_kl):
            s = islot((kl + n_kl - d) % n_kl, ly)
            got(chunk(buf, s, h), ids[("iz", a)] + d * CHUNKS + h)
            for e in range(1, n_ly):
                q = ids[("iy", a)] + (e * n_kl + d) * CHUNKS + h
                send(chunk(buf, s, h), chunk(buf, s, h), q, q, dev(ly_=(ly + e) % n_ly))

    def image_finish(a, buf):
        for h in range(CHUNKS):
            for e in range(1, n_ly):
                for d in range(n_kl):
                    s = islot((kl + n_kl - d) % n_kl, (ly + n_ly - e) % n_ly)
                    got(chunk(buf, s, h), ids[("iy", a)] + (e * n_kl + d) * CHUNKS + h)

    def text_first_copy(a, own, buf, h, g):
        dest = g * n_kl + src_kl
        q = ids[("tz", a)]
        s = tslot(src_j, lx, c)
        op = copy(chunk(own, 0, h), chunk(buf, s, h), q + g * CHUNKS + h,
                  q + src_j * CHUNKS + h, dev(k_=dest))
        return dest, op

    def text_first(a, own, buf, h):
        for g in range(n_kh):
            dest, op = text_first_copy(a, own, buf, h, g)

            @pl.when(dest != k)
            def _():
                op.start()

            @pl.when(dest == k)
            def _():
                o = pl.multiple_of(tslot(src_j, lx, c) * D + h * Dc, Dc)
                buf[pl.ds(o, Dc), :] = own[pl.ds(h * Dc, Dc), :]

    def text_first_drain(a, own, buf):
        for h in range(CHUNKS):
            for g in range(n_kh):
                dest, op = text_first_copy(a, own, buf, h, g)

                @pl.when(dest != k)
                def _():
                    op.wait_send()

    def text_relay(a, buf, h):
        for j in range(n_kh):
            s = tslot(j, lx, c)

            @pl.when(kl * n_kh + j != k)
            def _():
                got(chunk(buf, s, h), ids[("tz", a)] + j * CHUNKS + h)

            for e in range(1, n_lx):
                q = ids[("tx", a)] + (e * n_kh + j) * CHUNKS + h
                send(chunk(buf, s, h), chunk(buf, s, h), q, q, dev(lx_=(lx + e) % n_lx))
            q = ids[("tc", a)] + j * CHUNKS + h
            send(chunk(buf, s, h), chunk(buf, s, h), q, q, dev(c_=1 - c))

    def text_cross(a, buf, h):
        for e in range(1, n_lx):
            for j in range(n_kh):
                s = tslot(j, (lx + n_lx - e) % n_lx, c)
                got(chunk(buf, s, h), ids[("tx", a)] + (e * n_kh + j) * CHUNKS + h)
                q = ids[("tc", a)] + (e * n_kh + j) * CHUNKS + h
                send(chunk(buf, s, h), chunk(buf, s, h), q, q, dev(c_=1 - c))

    def text_finish(a, buf, e):
        for h in range(CHUNKS):
            for j in range(n_kh):
                s = tslot(j, (lx + n_lx - e) % n_lx, 1 - c)
                got(chunk(buf, s, h), ids[("tc", a)] + (e * n_kh + j) * CHUNKS + h)

    def teacher_wait(src, raw, base_id):
        raw[l] = src[at(l), :]
        for d in range(1, n_loop):
            got(raw.at[(l + n_loop - d) % n_loop], base_id + d)

    def teacher_unit(raw, dst, base, h):
        def body(i, _):
            o = pl.multiple_of(h * Dc + i * HALF, HALF)
            xs = [raw[f, pl.ds(o, HALF), :].astype(F32) for f in range(n_loop)]
            x = jnp.concatenate(xs, axis=1)
            _, inv = inv_norm(x)
            dst[pl.ds(pl.multiple_of(base + o, HALF), HALF), :] = (x * inv).astype(BF16)
            return 0
        lax.fori_loop(0, Dc // HALF, body, 0)

    a2a(tt, raw_t, ids["t_txt"])
    a2a(ti, raw_i, ids["t_img"])
    for h in range(CHUNKS):
        unit_to(st, own_s, 0, h)
        text_first(0, own_s, txt_s, h)
        unit_to(si, img_s, slot0 * D, h)
        image_first(0, img_s, h)
    for h in range(CHUNKS):
        text_relay(0, txt_s, h)
        image_relay(0, img_s, h)
        if h == 0:
            teacher_wait(tt, raw_t, ids["t_txt"])
        teacher_unit(raw_t, own_t, 0, h)
        text_first(1, own_t, txt_t, h)
        if h == 0:
            teacher_wait(ti, raw_i, ids["t_img"])
        teacher_unit(raw_i, img_t, slot0 * D, h)
        image_first(1, img_t, h)
    for h in range(CHUNKS):
        text_cross(0, txt_s, h)
        text_relay(1, txt_t, h)
        image_relay(1, img_t, h)
    image_finish(0, img_s)
    for e in range(n_lx):
        text_finish(0, txt_s, e)

    TILE = 2 * D

    def logits(txt, img, scale, out, e, m):
        def body(j, m):
            o = pl.multiple_of((j * n_lx + (lx + n_lx - e) % n_lx) * TILE, TILE)
            v = scale * lax.dot_general(
                txt[pl.ds(o, TILE), :], img[...], (((1,), (1,)), ((), ())),
                preferred_element_type=F32,
            )
            out[pl.ds(o, TILE), :] = v
            return jnp.maximum(m, jnp.max(v.reshape(TILE // 8, 8, rows), axis=0))
        return lax.fori_loop(0, n_kh, body, m)

    low = jnp.full((8, rows), -jnp.inf, F32)
    top = low
    for e in range(n_lx):
        top = logits(txt_s, img_s, sscale, slog, e, top)
    smax = jnp.max(top, axis=0, keepdims=True)
    for h in range(CHUNKS):
        text_cross(1, txt_t, h)
    image_finish(1, img_t)
    top = low
    for e in range(n_lx):
        text_finish(1, txt_t, e)
        top = logits(txt_t, img_t, tscale, tlog, e, top)
    tmax = jnp.max(top, axis=0, keepdims=True)

    def exps(i, carry):
        a, b, x = carry
        o = pl.multiple_of(i * STEP, STEP)
        s = slog[pl.ds(o, STEP), :]
        t = tlog[pl.ds(o, STEP), :]
        es = jnp.exp(s - smax)
        et = jnp.exp(t - tmax)
        slog[pl.ds(o, STEP), :] = es
        tlog[pl.ds(o, STEP), :] = et

        def fold(v):
            return jnp.sum(v.reshape(STEP // 8, 8, rows), axis=0)
        return (a + fold(es), b + fold(et), x + fold(et * (t - s)))

    zero = jnp.zeros((8, rows), F32)
    asum, bsum, xsum = lax.fori_loop(0, cols // STEP, exps, (zero, zero, zero))
    pack = [smax, tmax] + [jnp.sum(v, axis=0, keepdims=True) for v in (asum, bsum, xsum)]
    stat[slot0] = jnp.concatenate(pack + [jnp.zeros((3, rows), F32)], axis=0)
    for d in range(n_kl):
        for e in range(n_ly):
            if d or e:
                q = ids["stat"] + d * n_ly + e
                send(stat.at[slot0], stat.at[slot0], q, q,
                     dev(k_=kh * n_kl + (kl + d) % n_kl, ly_=(ly + e) % n_ly))
    for d in range(n_kl):
        for e in range(n_ly):
            if d or e:
                s = islot((kl + n_kl - d) % n_kl, (ly + n_ly - e) % n_ly)
                got(stat.at[s], ids["stat"] + d * n_ly + e)

    all_stat = [stat[s] for s in range(n_img)]
    gs = functools.reduce(jnp.maximum, [v[0:1] for v in all_stat])
    gt = functools.reduce(jnp.maximum, [v[1:2] for v in all_stat])
    es = [jnp.exp(v[0:1] - gs) for v in all_stat]
    et = [jnp.exp(v[1:2] - gt) for v in all_stat]
    ssum = sum(v[2:3] * e for v, e in zip(all_stat, es))
    tsum = sum(v[3:4] * e for v, e in zip(all_stat, et))
    cross = sum(v[4:5] * e for v, e in zip(all_stat, et))
    diverge = cross / tsum - (gt + jnp.log(tsum)) + (gs + jnp.log(ssum))
    s_mul = sscale * jnp.exp(smax - gs) / ssum
    t_mul = sscale * jnp.exp(tmax - gt) / tsum

    def to_grad(i, _):
        o = pl.multiple_of(i * STEP, STEP)
        v = slog[pl.ds(o, STEP), :] * s_mul - tlog[pl.ds(o, STEP), :] * t_mul
        grad[pl.ds(o, STEP), :] = v.astype(BF16)
        return 0
    lax.fori_loop(0, cols // STEP, to_grad, 0)

    drain()
    for a, own, buf in ((0, own_s, txt_s), (1, own_t, txt_t)):
        text_first_drain(a, own, buf)
    dtxt = txt_t

    def dtxt_pieces(lx_, c_):
        def body(j, _):
            rng = at(tslot(j, lx_, c_))
            dtxt[rng, :] = jnp.dot(grad[rng, :], img_s[...], preferred_element_type=F32).astype(BF16)
            return 0
        lax.fori_loop(0, n_kh, body, 0)

    def to_core(e):
        x_ = (lx + e) % n_lx
        dtxt_pieces(x_, 1 - c)
        for h in range(CHUNKS):
            for j in range(n_kh):
                q = ids["dc"] + (e * n_kh + j) * CHUNKS + h
                send(chunk(dtxt, tslot(j, x_, 1 - c), h), chunk_of(r1, x_ * n_kh + j, h), q, q, dev(c_=1 - c))

    def chunk_rows(slot, h):
        return pl.ds(pl.multiple_of(slot * D + h * Dc, Dc), Dc)

    half = [pl.ds(h * Dc, Dc) for h in range(CHUNKS)]

    for e in range(1, n_lx):
        x_ = (lx + e) % n_lx
        to_core(e)
        dtxt_pieces(x_, c)
        if e == n_lx - 1:
            to_core(0)
        for h in range(CHUNKS):
            for j in range(n_kh):
                i = x_ * n_kh + j
                got(chunk_of(r1, i, h), ids["dc"] + (e * n_kh + j) * CHUNKS + h)
                rng = chunk_rows(tslot(j, x_, c), h)
                dtxt[rng, :] = (dtxt[rng, :].astype(F32) + r1[i, half[h], :].astype(F32)).astype(BF16)
                q = ids["dx"] + (e * n_kh + j) * CHUNKS + h
                send(chunk(dtxt, tslot(j, x_, c), h), chunk_of(r2, (e - 1) * n_kh + j, h), q, q, dev(lx_=x_))

    dtxt_pieces(lx, c)

    KT = 256
    dimg_acc[...] = jnp.zeros_like(dimg_acc)

    def dimg_body(i, _):
        o = pl.multiple_of(i * KT, KT)
        dimg_acc[...] += lax.dot_general(
            grad[pl.ds(o, KT), :], txt_s[pl.ds(o, KT), :], (((0,), (0,)), ((), ())),
            preferred_element_type=F32,
        )
        return 0
    lax.fori_loop(0, cols // KT, dimg_body, 0)
    dimg = img_t
    for s in range(n_img):
        dimg[pl.ds(s * D, D), :] = dimg_acc[pl.ds(s * D, D), :].astype(BF16)
    for d in [*range(1, n_kl), 0]:
        for h in range(CHUNKS):
            for e in range(1, n_ly):
                y_ = (ly + e) % n_ly
                q = ids["gy"] + (e * n_kl + d) * CHUNKS + h
                send(chunk(dimg, islot((kl + d) % n_kl, y_), h), chunk_of(ry, (e - 1) * n_kl + d, h), q, q, dev(ly_=y_))


    def owner_copy(j, h):
        dest = kl * n_kh + j
        op = copy(chunk(dtxt, tslot(j, lx, c), h), chunk_of(r3, kh, h),
                  ids["dz"] + j * CHUNKS + h, ids["dz"] + kh * CHUNKS + h, dev(k_=dest))
        return dest, op

    def text_sum(j, h):
        got(chunk_of(r1, lx * n_kh + j, h), ids["dc"] + j * CHUNKS + h)
        rng = chunk_rows(tslot(j, lx, c), h)
        v = dtxt[rng, :].astype(F32) + r1[lx * n_kh + j, half[h], :].astype(F32)
        for e in range(1, n_lx):
            got(chunk_of(r2, (e - 1) * n_kh + j, h), ids["dx"] + (e * n_kh + j) * CHUNKS + h)
            v = v + r2[(e - 1) * n_kh + j, half[h], :].astype(F32)
        dtxt[rng, :] = v.astype(BF16)
        dest, op = owner_copy(j, h)

        @pl.when(dest != k)
        def _():
            op.start()

        @pl.when(dest == k)
        def _():
            r3[kh, half[h], :] = dtxt[rng, :]

    def got_y(d, h):
        for e in range(1, n_ly):
            got(chunk_of(ry, (e - 1) * n_kl + d, h), ids["gy"] + (e * n_kl + d) * CHUNKS + h)

    def image_sum(d, h):
        got_y(d, h)
        pair_slot = islot((kl + d) % n_kl, ly)
        rng = chunk_rows(pair_slot, h)
        v = dimg[rng, :].astype(F32)
        for e in range(1, n_ly):
            v = v + ry[(e - 1) * n_kl + d, half[h], :].astype(F32)
        dimg[rng, :] = v.astype(BF16)
        q = ids["gz"] + d * CHUNKS + h
        send(chunk(dimg, pair_slot, h), chunk_of(rz, d - 1, h), q, q, dev(k_=kh * n_kl + (kl + d) % n_kl))

    for h in range(CHUNKS):
        for j in range(n_kh):
            text_sum(j, h)
        for d in range(1, n_kl):
            image_sum(d, h)
    for h in range(CHUNKS):
        got_y(0, h)

    total = jnp.broadcast_to(jnp.sum(diverge, axis=1, keepdims=True), (8, 128))
    part[kh] = total
    for d in range(1, n_kh):
        q = ids["lk"] + d
        send(part.at[kh], part.at[kh], q, q, dev(k_=((kh + d) % n_kh) * n_kl + kl))
    for d in range(1, n_kh):
        got(part.at[(kh + n_kh - d) % n_kh], ids["lk"] + d)
    base = n_kh
    total = sum(part[i] for i in range(n_kh))
    part[base + lx] = total
    for d in range(1, n_lx):
        q = ids["lx"] + d
        send(part.at[base + lx], part.at[base + lx], q, q, dev(lx_=(lx + d) % n_lx))
    for d in range(1, n_lx):
        got(part.at[base + (lx + n_lx - d) % n_lx], ids["lx"] + d)
    total = sum(part[base + i] for i in range(n_lx))
    base = n_kh + n_lx
    part[base + c] = total
    send(part.at[base + c], part.at[base + c], ids["lc"], ids["lc"], dev(c_=1 - c))
    got(part.at[base + 1 - c], ids["lc"])
    total = part[base] + part[base + 1]
    loss_out[...] = total / float(D * n_row * n_loop)

    def add_terms(terms, out):
        def body(i, _):
            rng = pl.ds(pl.multiple_of(i * HALF, HALF), HALF)
            out[rng, :] = terms(rng)
            return 0
        lax.fori_loop(0, D // HALF, body, 0)

    for d in range(1, n_kl):
        for h in range(CHUNKS):
            got(chunk_of(rz, d - 1, h), ids["gz"] + d * CHUNKS + h)

    def image_terms(rng):
        o = pl.multiple_of(slot0 * D + rng.start, HALF)
        v = dimg[pl.ds(o, HALF), :].astype(F32)
        for e in range(1, n_ly):
            v = v + ry[(e - 1) * n_kl, rng, :].astype(F32)
        for d in range(1, n_kl):
            v = v + rz[d - 1, rng, :].astype(F32)
        return v
    add_terms(image_terms, gi_out)

    for g in range(n_kh):
        @pl.when(g * n_kl + src_kl != k)
        def _():
            for h in range(CHUNKS):
                got(chunk_of(r3, g, h), ids["dz"] + g * CHUNKS + h)
    add_terms(lambda rng: sum(r3[g, rng, :].astype(F32) for g in range(n_kh)), gt_out)

    drain()
    for j in range(n_kh):
        for h in range(CHUNKS):
            dest, op = owner_copy(j, h)

            @pl.when(dest != k)
            def _():
                op.wait_send()


def back_norms(si, st, total, di, dt, loss_out, gi_out, gt_out):
    loss_out[0] = total[0, 0]
    D = si.shape[0]
    block = 32 if D % 32 == 0 else 16

    def body(i, _):
        rng = pl.ds(pl.multiple_of(i * block, block), block)
        for src, grad_unit, out in ((si, di, gi_out), (st, dt, gt_out)):
            x = src[rng, :].astype(F32)
            g = grad_unit[rng, :]
            inv = 1.0 / jnp.sqrt(jnp.sum(x * x, axis=1, keepdims=True) + EPS)
            along = jnp.sum(g * x, axis=1, keepdims=True) * inv * inv
            out[rng, :] = ((g - x * along) * inv).astype(BF16)
        return 0
    lax.fori_loop(0, D // block, body, 0, unroll=True)


def on_device(n_row, n_loop, si, st, ti, tt, ssc, tsc):
    D, code = si.shape
    n_kl, n_lx = 2, 2
    n_kh, n_ly = n_row // (2 * n_kl), n_loop // n_lx
    n_img, n_txt = n_kl * n_ly, n_kh * n_lx * 2
    rows, cols = n_img * D, n_txt * D
    ids = make_ids(n_loop, n_kh, n_kl, n_lx, n_ly)
    dims = (n_row, n_loop, n_kh, n_kl, n_lx, n_ly, D, code)
    vm = pl.BlockSpec(memory_space=pltpu.VMEM)
    sm = pl.BlockSpec(memory_space=pltpu.SMEM)
    V = pltpu.VMEM
    loss, gi, gt = pl.pallas_call(
        functools.partial(kernel, dims, ids),
        out_shape=(
            jax.ShapeDtypeStruct((8, 128), F32),
            jax.ShapeDtypeStruct((D, code), F32),
            jax.ShapeDtypeStruct((D, code), F32),
        ),
        in_specs=[vm] * 4 + [sm] * 2,
        out_specs=(vm, vm, vm),
        scratch_shapes=[
            V((rows, code), BF16), V((rows, code), BF16),
            V((D, code), BF16), V((D, code), BF16),
            V((cols, code), BF16), V((cols, code), BF16),
            V((n_loop, D, code // n_loop), BF16), V((n_loop, D, code // n_loop), BF16),
            V((cols, rows), F32), V((cols, rows), F32), V((cols, rows), BF16),
            V((n_img, 8, rows), F32),
            V((rows, code), F32),
            V((n_lx * n_kh, D, code), BF16),
            V(((n_lx - 1) * n_kh, D, code), BF16),
            V((n_kh, D, code), BF16),
            V(((n_ly - 1) * n_kl, D, code), BF16),
            V((n_kl - 1, D, code), BF16),
            V((n_kh + n_lx + 2, 8, 128), F32),
            pltpu.SemaphoreType.DMA((ids.count,)),
            pltpu.SemaphoreType.DMA((ids.count,)),
        ],
        compiler_params=pltpu.CompilerParams(
            collective_id=0, has_side_effects=True, vmem_limit_bytes=67043328,
        ),
    )(si, st, ti, tt, ssc, tsc)
    return pl.pallas_call(
        back_norms,
        out_shape=(
            jax.ShapeDtypeStruct((1,), F32),
            jax.ShapeDtypeStruct((D, code), BF16),
            jax.ShapeDtypeStruct((D, code), BF16),
        ),
        in_specs=[vm] * 5,
        out_specs=(sm, vm, vm),
    )(si, st, loss, gi, gt)


def solution(mesh):
    return jax.shard_map(
        functools.partial(on_device, mesh.shape["row"], mesh.shape["loop"]),
        mesh=mesh,
        in_specs=(
            P(("row", "loop"), None),
            P(("row", "loop"), None),
            P("row", "loop"),
            P("row", "loop"),
            P(),
            P(),
        ),
        out_specs=(P(), P(("row", "loop"), None), P(("row", "loop"), None)),
        check_vma=False,
    )
```

```python
import functools
import jax
import jax.numpy as jnp
from jax import lax
from jax.experimental import pallas as pl
from jax.experimental.pallas import tpu as pltpu
from jax.sharding import PartitionSpec as P

EPS = 1e-06
F32 = jnp.float32
BF16 = jnp.bfloat16
MESH = pl.DeviceIdType.MESH
STEP = 32
CHUNKS = 2


class Ids:
    def __init__(self):
        self.table = {}
        self.count = 0

    def take(self, name, size=1):
        self.table[name] = self.count
        self.count += size

    def __getitem__(self, name):
        return self.table[name]


def make_ids(n_loop, n_kh, n_kl, n_lx, n_ly):
    ids = Ids()
    ids.take("t_img", n_loop)
    ids.take("t_txt", n_loop)
    for a in range(2):
        ids.take(("iz", a), n_kl * CHUNKS)
        ids.take(("iy", a), n_ly * n_kl * CHUNKS)
        ids.take(("tz", a), n_kh * CHUNKS)
        ids.take(("tx", a), n_lx * n_kh * CHUNKS)
        ids.take(("tc", a), n_lx * n_kh * CHUNKS)
    ids.take("stat", n_kl * n_ly)
    ids.take("dc", n_lx * n_kh * CHUNKS)
    ids.take("dx", n_lx * n_kh * CHUNKS)
    ids.take("dz", n_kh * CHUNKS)
    ids.take("gy", n_ly * n_kl * CHUNKS)
    ids.take("gz", n_kl * CHUNKS)
    ids.take("lk", n_kh)
    ids.take("lx", n_lx)
    ids.take("lc", 1)
    return ids


def kernel(
    dims, ids,
    si, st, ti, tt, ssc, tsc,
    loss_out, gi_out, gt_out,
    img_s, img_t, own_s, own_t, txt_s, txt_t, raw_i, raw_t,
    slog, tlog, grad, stat, dimg_acc, r1, r2, r3, ry, rz, part,
    ss, rs,
):
    n_row, n_loop, n_kh, n_kl, n_lx, n_ly, D, code = dims
    n_img = n_kl * n_ly
    n_txt = n_kh * n_lx * 2
    rows = n_img * D
    Dc = D // CHUNKS
    cols = n_txt * D
    feat = code // n_loop
    r = lax.axis_index("row")
    l = lax.axis_index("loop")
    k, c = r // 2, r % 2
    kh, kl = k // n_kl, k % n_kl
    src_kl, src_j = k // n_kh, k % n_kh
    ly, lx = l // n_lx, l % n_lx
    sscale = ssc[0]
    tscale = tsc[0]

    def dev(k_=None, c_=None, ly_=None, lx_=None):
        kk = k if k_ is None else k_
        cc = c if c_ is None else c_
        yy = ly if ly_ is None else ly_
        xx = lx if lx_ is None else lx_
        return (kk * 2 + cc, yy * n_lx + xx)

    def piece(ref, slot):
        return ref.at[pl.ds(pl.multiple_of(slot * D, D), D), :]

    def chunk(ref, slot, h):
        return ref.at[pl.ds(pl.multiple_of(slot * D + h * Dc, Dc), Dc), :]

    def chunk_of(ref, i, h):
        return ref.at[i, pl.ds(h * Dc, Dc), :]

    def at(slot):
        return pl.ds(pl.multiple_of(slot * D, D), D)

    def copy(src, dst, q_send, q_recv, device):
        return pltpu.make_async_remote_copy(
            src_ref=src, dst_ref=dst, send_sem=ss.at[q_send], recv_sem=rs.at[q_recv],
            device_id=device, device_id_type=MESH,
        )

    sent = []

    def send(src, dst, q_send, q_recv, device):
        op = copy(src, dst, q_send, q_recv, device)
        op.start()
        sent.append(op)

    def got(dst, q):
        copy(dst, dst, q, q, dev(c_=1 - c)).wait_recv()

    def drain():
        for op in sent:
            op.wait_send()
        sent.clear()

    barrier = pltpu.get_barrier_semaphore()
    n_peer = 0
    for d in range(1, n_loop):
        pl.semaphore_signal(barrier, inc=1, device_id=(r, (l + d) % n_loop), device_id_type=MESH)
        n_peer += 1
    for d in range(1, n_kh * n_kl):
        pl.semaphore_signal(barrier, inc=1, device_id=dev(k_=(k + d) % (n_kh * n_kl)), device_id_type=MESH)
        n_peer += 1
    pl.semaphore_signal(barrier, inc=1, device_id=dev(c_=1 - c), device_id_type=MESH)
    n_peer += 1
    for d in range(1, n_kl):
        for e in range(1, n_ly):
            diagonal = dev(k_=kh * n_kl + (kl + d) % n_kl, ly_=(ly + e) % n_ly)
            pl.semaphore_signal(barrier, inc=1, device_id=diagonal, device_id_type=MESH)
            n_peer += 1
    pl.semaphore_wait(barrier, n_peer)

    slot0 = kl * n_ly + ly

    def islot(kl_, ly_):
        return kl_ * n_ly + ly_

    def tslot(j, lx_, c_):
        return (j * n_lx + lx_) * 2 + c_

    def inv_norm(x):
        n2 = jnp.sum(x * x, axis=1, keepdims=True) + EPS
        n = jnp.sqrt(n2)
        return n, 1.0 / n

    HALF = Dc if Dc <= 80 else 16

    def unit_to(src, dst, base, h):
        def body(i, _):
            o = pl.multiple_of(h * Dc + i * HALF, HALF)
            x = src[pl.ds(o, HALF), :].astype(F32)
            _, inv = inv_norm(x)
            dst[pl.ds(pl.multiple_of(base + o, HALF), HALF), :] = (x * inv).astype(BF16)
            return 0
        lax.fori_loop(0, Dc // HALF, body, 0)

    def a2a(src, raw, base):
        for d in range(1, n_loop):
            peer = (l + d) % n_loop
            send(piece(src, peer), raw.at[l], base + d, base + d, (r, peer))

    def image_first(a, buf, h):
        for d in range(1, n_kl):
            p = (kl + d) % n_kl
            q = ids[("iz", a)] + d * CHUNKS + h
            send(chunk(buf, slot0, h), chunk(buf, slot0, h), q, q, dev(k_=kh * n_kl + p))
        for e in range(1, n_ly):
            q = ids[("iy", a)] + e * n_kl * CHUNKS + h
            send(chunk(buf, slot0, h), chunk(buf, slot0, h), q, q, dev(ly_=(ly + e) % n_ly))

    def image_relay(a, buf, h):
        for d in range(1, n_kl):
            s = islot((kl + n_kl - d) % n_kl, ly)
            got(chunk(buf, s, h), ids[("iz", a)] + d * CHUNKS + h)
            for e in range(1, n_ly):
                q = ids[("iy", a)] + (e * n_kl + d) * CHUNKS + h
                send(chunk(buf, s, h), chunk(buf, s, h), q, q, dev(ly_=(ly + e) % n_ly))

    def image_finish(a, buf):
        for h in range(CHUNKS):
            for e in range(1, n_ly):
                for d in range(n_kl):
                    s = islot((kl + n_kl - d) % n_kl, (ly + n_ly - e) % n_ly)
                    got(chunk(buf, s, h), ids[("iy", a)] + (e * n_kl + d) * CHUNKS + h)

    def text_first_copy(a, own, buf, h, g):
        dest = g * n_kl + src_kl
        q = ids[("tz", a)]
        s = tslot(src_j, lx, c)
        op = copy(chunk(own, 0, h), chunk(buf, s, h), q + g * CHUNKS + h,
                  q + src_j * CHUNKS + h, dev(k_=dest))
        return dest, op

    def text_first(a, own, buf, h):
        for g in range(n_kh):
            dest, op = text_first_copy(a, own, buf, h, g)

            @pl.when(dest != k)
            def _():
                op.start()

            @pl.when(dest == k)
            def _():
                o = pl.multiple_of(tslot(src_j, lx, c) * D + h * Dc, Dc)
                buf[pl.ds(o, Dc), :] = own[pl.ds(h * Dc, Dc), :]

    def text_first_drain(a, own, buf):
        for h in range(CHUNKS):
            for g in range(n_kh):
                dest, op = text_first_copy(a, own, buf, h, g)

                @pl.when(dest != k)
                def _():
                    op.wait_send()

    def text_relay(a, buf, h):
        for j in range(n_kh):
            s = tslot(j, lx, c)

            @pl.when(kl * n_kh + j != k)
            def _():
                got(chunk(buf, s, h), ids[("tz", a)] + j * CHUNKS + h)

            for e in range(1, n_lx):
                q = ids[("tx", a)] + (e * n_kh + j) * CHUNKS + h
                send(chunk(buf, s, h), chunk(buf, s, h), q, q, dev(lx_=(lx + e) % n_lx))
            q = ids[("tc", a)] + j * CHUNKS + h
            send(chunk(buf, s, h), chunk(buf, s, h), q, q, dev(c_=1 - c))

    def text_cross(a, buf, h):
        for e in range(1, n_lx):
            for j in range(n_kh):
                s = tslot(j, (lx + n_lx - e) % n_lx, c)
                got(chunk(buf, s, h), ids[("tx", a)] + (e * n_kh + j) * CHUNKS + h)
                q = ids[("tc", a)] + (e * n_kh + j) * CHUNKS + h
                send(chunk(buf, s, h), chunk(buf, s, h), q, q, dev(c_=1 - c))

    def text_finish(a, buf, e):
        for h in range(CHUNKS):
            for j in range(n_kh):
                s = tslot(j, (lx + n_lx - e) % n_lx, 1 - c)
                got(chunk(buf, s, h), ids[("tc", a)] + (e * n_kh + j) * CHUNKS + h)

    def teacher_wait(src, raw, base_id):
        raw[l] = src[at(l), :]
        for d in range(1, n_loop):
            got(raw.at[(l + n_loop - d) % n_loop], base_id + d)

    def teacher_unit(raw, dst, base, h):
        def body(i, _):
            o = pl.multiple_of(h * Dc + i * HALF, HALF)
            xs = [raw[f, pl.ds(o, HALF), :].astype(F32) for f in range(n_loop)]
            x = jnp.concatenate(xs, axis=1)
            _, inv = inv_norm(x)
            dst[pl.ds(pl.multiple_of(base + o, HALF), HALF), :] = (x * inv).astype(BF16)
            return 0
        lax.fori_loop(0, Dc // HALF, body, 0)

    a2a(tt, raw_t, ids["t_txt"])
    a2a(ti, raw_i, ids["t_img"])
    for h in range(CHUNKS):
        unit_to(st, own_s, 0, h)
        text_first(0, own_s, txt_s, h)
        unit_to(si, img_s, slot0 * D, h)
        image_first(0, img_s, h)
    for h in range(CHUNKS):
        if h == 0:
            text_relay(0, txt_s, h)
            image_relay(0, img_s, h)
            teacher_wait(tt, raw_t, ids["t_txt"])
        teacher_unit(raw_t, own_t, 0, h)
        text_first(1, own_t, txt_t, h)
        if h == 0:
            teacher_wait(ti, raw_i, ids["t_img"])
        teacher_unit(raw_i, img_t, slot0 * D, h)
        image_first(1, img_t, h)
    for h in range(1, CHUNKS):
        text_relay(0, txt_s, h)
        image_relay(0, img_s, h)
    for h in range(CHUNKS):
        text_cross(0, txt_s, h)
        text_relay(1, txt_t, h)
        image_relay(1, img_t, h)
    image_finish(0, img_s)
    for e in range(n_lx):
        text_finish(0, txt_s, e)

    TILE = 2 * D

    def logits(txt, img, scale, out, e, m):
        def body(j, m):
            o = pl.multiple_of((j * n_lx + (lx + n_lx - e) % n_lx) * TILE, TILE)
            v = scale * lax.dot_general(
                txt[pl.ds(o, TILE), :], img[...], (((1,), (1,)), ((), ())),
                preferred_element_type=F32,
            )
            out[pl.ds(o, TILE), :] = v
            return jnp.maximum(m, jnp.max(v.reshape(TILE // 8, 8, rows), axis=0))
        return lax.fori_loop(0, n_kh, body, m)

    low = jnp.full((8, rows), -jnp.inf, F32)
    top = low
    for e in range(n_lx):
        top = logits(txt_s, img_s, sscale, slog, e, top)
    smax = jnp.max(top, axis=0, keepdims=True)
    for h in range(CHUNKS):
        text_cross(1, txt_t, h)
    image_finish(1, img_t)
    top = low
    for e in range(n_lx):
        text_finish(1, txt_t, e)
        top = logits(txt_t, img_t, tscale, tlog, e, top)
    tmax = jnp.max(top, axis=0, keepdims=True)

    def exps(i, carry):
        a, b, x = carry
        o = pl.multiple_of(i * STEP, STEP)
        s = slog[pl.ds(o, STEP), :]
        t = tlog[pl.ds(o, STEP), :]
        es = jnp.exp(s - smax)
        et = jnp.exp(t - tmax)
        slog[pl.ds(o, STEP), :] = es
        tlog[pl.ds(o, STEP), :] = et

        def fold(v):
            return jnp.sum(v.reshape(STEP // 8, 8, rows), axis=0)
        return (a + fold(es), b + fold(et), x + fold(et * (t - s)))

    zero = jnp.zeros((8, rows), F32)
    asum, bsum, xsum = lax.fori_loop(0, cols // STEP, exps, (zero, zero, zero))
    pack = [smax, tmax] + [jnp.sum(v, axis=0, keepdims=True) for v in (asum, bsum, xsum)]
    stat[slot0] = jnp.concatenate(pack + [jnp.zeros((3, rows), F32)], axis=0)
    for d in range(n_kl):
        for e in range(n_ly):
            if d or e:
                q = ids["stat"] + d * n_ly + e
                send(stat.at[slot0], stat.at[slot0], q, q,
                     dev(k_=kh * n_kl + (kl + d) % n_kl, ly_=(ly + e) % n_ly))
    for d in range(n_kl):
        for e in range(n_ly):
            if d or e:
                s = islot((kl + n_kl - d) % n_kl, (ly + n_ly - e) % n_ly)
                got(stat.at[s], ids["stat"] + d * n_ly + e)

    all_stat = [stat[s] for s in range(n_img)]
    gs = functools.reduce(jnp.maximum, [v[0:1] for v in all_stat])
    gt = functools.reduce(jnp.maximum, [v[1:2] for v in all_stat])
    es = [jnp.exp(v[0:1] - gs) for v in all_stat]
    et = [jnp.exp(v[1:2] - gt) for v in all_stat]
    ssum = sum(v[2:3] * e for v, e in zip(all_stat, es))
    tsum = sum(v[3:4] * e for v, e in zip(all_stat, et))
    cross = sum(v[4:5] * e for v, e in zip(all_stat, et))
    diverge = cross / tsum - (gt + jnp.log(tsum)) + (gs + jnp.log(ssum))
    s_mul = sscale * jnp.exp(smax - gs) / ssum
    t_mul = sscale * jnp.exp(tmax - gt) / tsum

    def to_grad(i, _):
        o = pl.multiple_of(i * STEP, STEP)
        v = slog[pl.ds(o, STEP), :] * s_mul - tlog[pl.ds(o, STEP), :] * t_mul
        grad[pl.ds(o, STEP), :] = v.astype(BF16)
        return 0
    lax.fori_loop(0, cols // STEP, to_grad, 0)

    drain()
    for a, own, buf in ((0, own_s, txt_s), (1, own_t, txt_t)):
        text_first_drain(a, own, buf)
    dtxt = txt_t

    def dtxt_pieces(lx_, c_):
        def body(j, _):
            rng = at(tslot(j, lx_, c_))
            dtxt[rng, :] = jnp.dot(grad[rng, :], img_s[...], preferred_element_type=F32).astype(BF16)
            return 0
        lax.fori_loop(0, n_kh, body, 0)

    def to_core(e):
        x_ = (lx + e) % n_lx
        dtxt_pieces(x_, 1 - c)
        for h in range(CHUNKS):
            for j in range(n_kh):
                q = ids["dc"] + (e * n_kh + j) * CHUNKS + h
                send(chunk(dtxt, tslot(j, x_, 1 - c), h), chunk_of(r1, x_ * n_kh + j, h), q, q, dev(c_=1 - c))

    def chunk_rows(slot, h):
        return pl.ds(pl.multiple_of(slot * D + h * Dc, Dc), Dc)

    half = [pl.ds(h * Dc, Dc) for h in range(CHUNKS)]

    for e in range(1, n_lx):
        x_ = (lx + e) % n_lx
        to_core(e)
        dtxt_pieces(x_, c)
        if e == n_lx - 1:
            to_core(0)
        for h in range(CHUNKS):
            for j in range(n_kh):
                i = x_ * n_kh + j
                got(chunk_of(r1, i, h), ids["dc"] + (e * n_kh + j) * CHUNKS + h)
                rng = chunk_rows(tslot(j, x_, c), h)
                dtxt[rng, :] = (dtxt[rng, :].astype(F32) + r1[i, half[h], :].astype(F32)).astype(BF16)
                q = ids["dx"] + (e * n_kh + j) * CHUNKS + h
                send(chunk(dtxt, tslot(j, x_, c), h), chunk_of(r2, (e - 1) * n_kh + j, h), q, q, dev(lx_=x_))

    KT = 256
    dimg_acc[...] = jnp.zeros_like(dimg_acc)

    def dimg_body(i, _):
        o = pl.multiple_of(i * KT, KT)
        dimg_acc[...] += lax.dot_general(
            grad[pl.ds(o, KT), :], txt_s[pl.ds(o, KT), :], (((0,), (0,)), ((), ())),
            preferred_element_type=F32,
        )
        return 0
    lax.fori_loop(0, cols // KT, dimg_body, 0)
    dimg = img_t
    for s in range(n_img):
        dimg[pl.ds(s * D, D), :] = dimg_acc[pl.ds(s * D, D), :].astype(BF16)
    for d in [*range(1, n_kl), 0]:
        for h in range(CHUNKS):
            for e in range(1, n_ly):
                y_ = (ly + e) % n_ly
                q = ids["gy"] + (e * n_kl + d) * CHUNKS + h
                send(chunk(dimg, islot((kl + d) % n_kl, y_), h), chunk_of(ry, (e - 1) * n_kl + d, h), q, q, dev(ly_=y_))


    dtxt_pieces(lx, c)

    def owner_copy(j, h):
        dest = kl * n_kh + j
        op = copy(chunk(dtxt, tslot(j, lx, c), h), chunk_of(r3, kh, h),
                  ids["dz"] + j * CHUNKS + h, ids["dz"] + kh * CHUNKS + h, dev(k_=dest))
        return dest, op

    def text_sum(j, h):
        got(chunk_of(r1, lx * n_kh + j, h), ids["dc"] + j * CHUNKS + h)
        rng = chunk_rows(tslot(j, lx, c), h)
        v = dtxt[rng, :].astype(F32) + r1[lx * n_kh + j, half[h], :].astype(F32)
        for e in range(1, n_lx):
            got(chunk_of(r2, (e - 1) * n_kh + j, h), ids["dx"] + (e * n_kh + j) * CHUNKS + h)
            v = v + r2[(e - 1) * n_kh + j, half[h], :].astype(F32)
        dtxt[rng, :] = v.astype(BF16)
        dest, op = owner_copy(j, h)

        @pl.when(dest != k)
        def _():
            op.start()

        @pl.when(dest == k)
        def _():
            r3[kh, half[h], :] = dtxt[rng, :]

    def got_y(d, h):
        for e in range(1, n_ly):
            got(chunk_of(ry, (e - 1) * n_kl + d, h), ids["gy"] + (e * n_kl + d) * CHUNKS + h)

    def image_sum(d, h):
        got_y(d, h)
        pair_slot = islot((kl + d) % n_kl, ly)
        rng = chunk_rows(pair_slot, h)
        v = dimg[rng, :].astype(F32)
        for e in range(1, n_ly):
            v = v + ry[(e - 1) * n_kl + d, half[h], :].astype(F32)
        dimg[rng, :] = v.astype(BF16)
        q = ids["gz"] + d * CHUNKS + h
        send(chunk(dimg, pair_slot, h), chunk_of(rz, d - 1, h), q, q, dev(k_=kh * n_kl + (kl + d) % n_kl))

    for h in range(CHUNKS):
        for j in range(n_kh):
            text_sum(j, h)
        for d in range(1, n_kl):
            image_sum(d, h)
    for h in range(CHUNKS):
        got_y(0, h)

    total = jnp.broadcast_to(jnp.sum(diverge, axis=1, keepdims=True), (8, 128))
    part[kh] = total
    for d in range(1, n_kh):
        q = ids["lk"] + d
        send(part.at[kh], part.at[kh], q, q, dev(k_=((kh + d) % n_kh) * n_kl + kl))
    for d in range(1, n_kh):
        got(part.at[(kh + n_kh - d) % n_kh], ids["lk"] + d)
    base = n_kh
    total = sum(part[i] for i in range(n_kh))
    part[base + lx] = total
    for d in range(1, n_lx):
        q = ids["lx"] + d
        send(part.at[base + lx], part.at[base + lx], q, q, dev(lx_=(lx + d) % n_lx))
    for d in range(1, n_lx):
        got(part.at[base + (lx + n_lx - d) % n_lx], ids["lx"] + d)
    total = sum(part[base + i] for i in range(n_lx))
    base = n_kh + n_lx
    part[base + c] = total
    send(part.at[base + c], part.at[base + c], ids["lc"], ids["lc"], dev(c_=1 - c))
    got(part.at[base + 1 - c], ids["lc"])
    total = part[base] + part[base + 1]
    loss_out[...] = total / float(D * n_row * n_loop)

    def add_terms(terms, out):
        def body(i, _):
            rng = pl.ds(pl.multiple_of(i * HALF, HALF), HALF)
            out[rng, :] = terms(rng)
            return 0
        lax.fori_loop(0, D // HALF, body, 0)

    for d in range(1, n_kl):
        for h in range(CHUNKS):
            got(chunk_of(rz, d - 1, h), ids["gz"] + d * CHUNKS + h)

    def image_terms(rng):
        o = pl.multiple_of(slot0 * D + rng.start, HALF)
        v = dimg[pl.ds(o, HALF), :].astype(F32)
        for e in range(1, n_ly):
            v = v + ry[(e - 1) * n_kl, rng, :].astype(F32)
        for d in range(1, n_kl):
            v = v + rz[d - 1, rng, :].astype(F32)
        return v
    add_terms(image_terms, gi_out)

    for g in range(n_kh):
        @pl.when(g * n_kl + src_kl != k)
        def _():
            for h in range(CHUNKS):
                got(chunk_of(r3, g, h), ids["dz"] + g * CHUNKS + h)
    add_terms(lambda rng: sum(r3[g, rng, :].astype(F32) for g in range(n_kh)), gt_out)

    drain()
    for j in range(n_kh):
        for h in range(CHUNKS):
            dest, op = owner_copy(j, h)

            @pl.when(dest != k)
            def _():
                op.wait_send()


def back_norms(si, st, total, di, dt, loss_out, gi_out, gt_out):
    loss_out[0] = total[0, 0]
    D = si.shape[0]
    block = 32 if D % 32 == 0 else 16

    def body(i, _):
        rng = pl.ds(pl.multiple_of(i * block, block), block)
        for src, grad_unit, out in ((si, di, gi_out), (st, dt, gt_out)):
            x = src[rng, :].astype(F32)
            g = grad_unit[rng, :]
            inv = 1.0 / jnp.sqrt(jnp.sum(x * x, axis=1, keepdims=True) + EPS)
            along = jnp.sum(g * x, axis=1, keepdims=True) * inv * inv
            out[rng, :] = ((g - x * along) * inv).astype(BF16)
        return 0
    lax.fori_loop(0, D // block, body, 0, unroll=True)


def on_device(n_row, n_loop, si, st, ti, tt, ssc, tsc):
    D, code = si.shape
    n_kl, n_lx = 2, 2
    n_kh, n_ly = n_row // (2 * n_kl), n_loop // n_lx
    n_img, n_txt = n_kl * n_ly, n_kh * n_lx * 2
    rows, cols = n_img * D, n_txt * D
    ids = make_ids(n_loop, n_kh, n_kl, n_lx, n_ly)
    dims = (n_row, n_loop, n_kh, n_kl, n_lx, n_ly, D, code)
    vm = pl.BlockSpec(memory_space=pltpu.VMEM)
    sm = pl.BlockSpec(memory_space=pltpu.SMEM)
    V = pltpu.VMEM
    loss, gi, gt = pl.pallas_call(
        functools.partial(kernel, dims, ids),
        out_shape=(
            jax.ShapeDtypeStruct((8, 128), F32),
            jax.ShapeDtypeStruct((D, code), F32),
            jax.ShapeDtypeStruct((D, code), F32),
        ),
        in_specs=[vm] * 4 + [sm] * 2,
        out_specs=(vm, vm, vm),
        scratch_shapes=[
            V((rows, code), BF16), V((rows, code), BF16),
            V((D, code), BF16), V((D, code), BF16),
            V((cols, code), BF16), V((cols, code), BF16),
            V((n_loop, D, code // n_loop), BF16), V((n_loop, D, code // n_loop), BF16),
            V((cols, rows), F32), V((cols, rows), F32), V((cols, rows), BF16),
            V((n_img, 8, rows), F32),
            V((rows, code), F32),
            V((n_lx * n_kh, D, code), BF16),
            V(((n_lx - 1) * n_kh, D, code), BF16),
            V((n_kh, D, code), BF16),
            V(((n_ly - 1) * n_kl, D, code), BF16),
            V((n_kl - 1, D, code), BF16),
            V((n_kh + n_lx + 2, 8, 128), F32),
            pltpu.SemaphoreType.DMA((ids.count,)),
            pltpu.SemaphoreType.DMA((ids.count,)),
        ],
        compiler_params=pltpu.CompilerParams(
            collective_id=0, has_side_effects=True, vmem_limit_bytes=67043328,
        ),
    )(si, st, ti, tt, ssc, tsc)
    return pl.pallas_call(
        back_norms,
        out_shape=(
            jax.ShapeDtypeStruct((1,), F32),
            jax.ShapeDtypeStruct((D, code), BF16),
            jax.ShapeDtypeStruct((D, code), BF16),
        ),
        in_specs=[vm] * 5,
        out_specs=(sm, vm, vm),
    )(si, st, loss, gi, gt)


def solution(mesh):
    return jax.shard_map(
        functools.partial(on_device, mesh.shape["row"], mesh.shape["loop"]),
        mesh=mesh,
        in_specs=(
            P(("row", "loop"), None),
            P(("row", "loop"), None),
            P("row", "loop"),
            P("row", "loop"),
            P(),
            P(),
        ),
        out_specs=(P(), P(("row", "loop"), None), P(("row", "loop"), None)),
        check_vma=False,
    )
```
